128 devices in a mesh: row: 8 (over y_hi, x), col: 16 (over y_lo, z, core).
Axes of the slice: x: 4, y: 4 (y_hi: 2, y_lo: 2; y = y_hi * 2 + y_lo), z: 4, core: 2. Of those that a mesh axis runs over, the one named last changes fastest.
Arguments:
- front_orig: float32 [12288, 12288], P('row', 'col')
- pivot_shift: float32 [12288], replicated, may hold values from 4.5 to 9
- child_update: float32 [16384, 8192], P('row', 'col'), may hold values from -0.046875 to 0.046875
- child_map: int32 [2, 32], replicated, may hold values from 0 to 47, as said below
Outputs:
- front_out: float32 [12288, 12288], P('row', 'col')
The draws below stay inside these ranges and needn't reach their ends.
Inputs may be any that keep to these rules, and one draw needn't show every extreme that they name: Child h's block b (rows and columns alike) goes to parent block child_map[h, b]; child_map[h, b] % 16 == b % 16; the two child blocks b and b + 16 (b < 16) take two different ones of the parent blocks b, b + 16, b + 32, the smaller child block to the smaller parent block.
All inputs are finite; a program needn't handle non-finite values.
Results may differ from the reference program's by a relative error of at most 0.0001.
Values sent between devices are 32-bit elements; how exact they have to be, the bound alone decides.
No kernel may reach another device: no remote copies, remote signals or barrier semaphores. Data moves between devices by JAX's collectives and lax.ppermute only.
A program may use at most 128 MiB of HBM per device.

```python
import jax
import jax.numpy as jnp
from jax import lax

BS = 256
PANELS = 6
CB = 32
F = 12288
C = 8192
N_ROW = 8
N_COL = 16


def draw_front_orig(key, part):
    spread = jnp.float32(F) ** (-0.5)
    values = jnp.abs(jnp.clip(jax.random.normal(key, (F, F), jnp.float32), -6.0, 6.0)) * spread
    return values.astype(jnp.float32)


def draw_child_map(key, part):
    residues = CB // 2
    skipped = jax.random.randint(key, (2, residues), 0, 3)
    opening = 1 + jax.random.randint(jax.random.fold_in(key, 11), (), 0, 2)
    closing = jax.random.randint(jax.random.fold_in(key, 12), (), 0, 2)
    skipped = skipped.at[0, 0].set(opening).at[0, residues - 1].set(closing)
    lower_slot = jnp.where(skipped == 0, 1, 0)
    upper_slot = jnp.where(skipped == 2, 1, 2)
    residue = jnp.arange(residues, dtype=jnp.int32)[None, :]
    first_half = residue + residues * lower_slot
    second_half = residue + residues * upper_slot
    return jnp.concatenate([first_half, second_half], axis=1).astype(jnp.int32)


def levels(own_key, dims, shards, smallest, largest):
    def one(axis_at, shards_of):
        draws = jax.random.uniform(jax.random.fold_in(jax.random.fold_in(own_key, 6), axis_at), (shards_of,), jnp.float32, smallest / len(shards), largest / len(shards))
        return jnp.repeat(jnp.exp(draws), dims[axis_at] // shards_of).reshape((-1,) + (1,) * (len(dims) - axis_at - 1))

    gain = one(*shards[0])
    for cut in shards[1:]:
        gain = gain * one(*cut)
    return gain


def scatter_about(own_key, extent, scale, reach, pieces=(), kind=jnp.bfloat16):
    values = jax.random.normal(own_key, extent, jnp.float32) * scale
    if len(pieces) > 0:
        values = levels(own_key, extent, pieces, -0.22, 0.18) * values
    return jnp.clip(values, min=-reach, max=reach).astype(kind)


def setup_inputs(seed: int = 0) -> dict:
    streams_of = jax.random.split(jax.random.key(seed), 5)
    front_orig = draw_front_orig(jax.random.fold_in(streams_of[4], 71), 0)
    pivot_shift = jnp.clip(jax.random.uniform(streams_of[1], (F,), jnp.float32, 4.5, 9.0), 4.5, 9.0)
    child_update = scatter_about(streams_of[2], (2 * C, C), (2 * C) ** -0.5, 0.046875, ((0, 8), (1, 16)), jnp.float32)
    child_map = draw_child_map(jax.random.fold_in(streams_of[4], 71), 0)
    return {"front_orig": front_orig, "pivot_shift": pivot_shift, "child_update": child_update, "child_map": child_map}


def natural_order(stored, rows_dev, cols_dev):
    total_rows, total_cols = stored.shape
    row_tiles = total_rows // BS // rows_dev
    col_tiles = total_cols // BS // cols_dev
    shaped = stored.reshape(rows_dev, row_tiles, BS, cols_dev, col_tiles, BS)
    return shaped.transpose(1, 0, 2, 4, 3, 5).reshape(total_rows, total_cols)

def storage_order(natural, rows_dev, cols_dev):
    total_rows, total_cols = natural.shape
    row_tiles = total_rows // BS // rows_dev
    col_tiles = total_cols // BS // cols_dev
    shaped = natural.reshape(row_tiles, rows_dev, BS, col_tiles, cols_dev, BS)
    return shaped.transpose(1, 0, 2, 4, 3, 5).reshape(total_rows, total_cols)

def symmetric_block(pivot_block):
    return jnp.tril(pivot_block) + jnp.tril(pivot_block, -1).T

def reference(front_orig, pivot_shift, child_update, child_map):
    front_now = natural_order(front_orig, N_ROW, N_COL)
    diagonal = jnp.arange(F, dtype=jnp.int32)
    front_now = front_now.at[diagonal, diagonal].add(pivot_shift)
    offsets = jnp.arange(BS, dtype=jnp.int32)
    for child_id in range(2):
        update = natural_order(child_update[child_id * C:(child_id + 1) * C], N_ROW // 2, N_COL)
        placement = (child_map[child_id].astype(jnp.int32)[:, None] * BS + offsets[None, :]).reshape(-1)
        front_now = front_now.at[placement[:, None], placement[None, :]].add(update)
    for panel_id in range(PANELS):
        first_row = panel_id * BS
        finish = first_row + BS
        factor = jnp.linalg.cholesky(symmetric_block(front_now[first_row:finish, first_row:finish]))
        below = lax.linalg.triangular_solve(factor, front_now[finish:, first_row:finish], left_side=False, lower=True, transpose_a=True)
        front_now = front_now.at[first_row:finish, first_row:finish].set(factor)
        front_now = front_now.at[finish:, first_row:finish].set(below)
        product = jnp.dot(below, below.T, precision=lax.Precision.HIGHEST)
        front_now = front_now.at[finish:, finish:].add(-product)
    return storage_order(front_now, N_ROW, N_COL)
```

```python
import jax
import jax.numpy as jnp
from jax import lax
from jax.experimental import pallas as pl
from jax.experimental.pallas import tpu as pltpu
from jax.sharding import PartitionSpec as P

PANELS = 6
BS=256
NT = (((1,), (1,)), ((), ()))
NN = (((1,), (0,)), ((), ()))

def split(x):
    hi = x.astype(jnp.bfloat16)
    return hi, (x - hi.astype(jnp.float32)).astype(jnp.bfloat16)

def dot(a, b, dims=NT):
    return lax.dot_general(a, b, dims, preferred_element_type=jnp.float32)

def dot3(ah, al, bh, bl, dims=NT):
    return dot(ah, bh, dims) + (dot(ah, bl, dims) + dot(al, bh, dims))

def mul3(a, b, dims=NT):
    return dot3(*split(a), *split(b), dims)

def leaf(sym):
    n = sym.shape[0]
    groups = n // 8
    lane = lax.broadcasted_iota(jnp.int32, (8, n), 1)
    sub = lax.broadcasted_iota(jnp.int32, (8, n), 0)
    across = lambda v, j: jnp.broadcast_to(v[:, j:j + 1], (8, n))
    down = lambda v, s: jnp.broadcast_to(v[s:s + 1, :], (8, n))
    rows = [sym[8 * h:8 * h + 8] for h in range(groups)]
    right = [jnp.where(lane == sub + 8 * h, 1.0, 0.0) for h in range(groups)]
    upper, inverse = [], []
    for g in range(groups):
        cols = [across(rows[g], 8 * g + t) for t in range(8)]
        a = {(s, t): down(cols[t], s) for t in range(8) for s in range(t, 8)}
        u = [down(rows[g], t) for t in range(8)]
        w = [down(right[g], t) for t in range(8)]
        later = range(g + 1, groups)
        x = {h: [across(rows[h], 8 * g + t) for t in range(8)] for h in later}
        for t in range(8):
            r = lax.rsqrt(a[t, t])
            for s in range(t + 1, 8):
                a[s, t] = a[s, t] * r
            u[t] = u[t] * r
            w[t] = w[t] * r
            for h in later:
                x[h][t] = x[h][t] * r
            for s in range(t + 1, 8):
                for v in range(t + 1, s + 1):
                    a[s, v] = a[s, v] - a[s, t] * a[v, t]
                u[s] = u[s] - a[s, t] * u[t]
                w[s] = w[s] - a[s, t] * w[t]
                for h in later:
                    x[h][s] = x[h][s] - a[s, t] * x[h][t]
        for h in later:
            for t in range(8):
                rows[h] = rows[h] - x[h][t] * u[t]
                right[h] = right[h] - x[h][t] * w[t]
        ug, wg = u[0], w[0]
        for t in range(1, 8):
            ug = jnp.where(sub == t, u[t], ug)
            wg = jnp.where(sub == t, w[t], wg)
        upper.append(jnp.where(lane >= sub + 8 * g, ug, 0.0))
        inverse.append(wg)
    return jnp.concatenate(upper, axis=0).T, jnp.concatenate(inverse, axis=0)

def symmetric(d):
    n = d.shape[0]
    below = lax.broadcasted_iota(jnp.int32, (n, n), 0) >= lax.broadcasted_iota(jnp.int32, (n, n), 1)
    return jnp.where(below, d, d.T)

LEAF = 128
def chol_kernel(panels, top_ref, lh_ref, ll_ref, ih_ref, il_ref, fac_ref, a_ref, s_ref, f_ref, w_ref):
    e = 0
    for i in range(panels):
        for k in range(i + 1):
            a_ref[k * panels + i] = top_ref[:, e].reshape(BS, BS)
            e += 1
    zero = jnp.zeros((LEAF, LEAF), jnp.float32)

    def panel(k, carry):
        d = a_ref[k * panels + k]
        s_ref[0] = d[:LEAF, :LEAF]
        s_ref[1] = d[LEAF:, LEAF:]
        s_ref[2] = d[LEAF:, :LEAF]

        def half(h, carry):
            factor, inverse = leaf(symmetric(s_ref[h]))
            f_ref[h] = factor
            w_ref[h] = inverse

            @pl.when(h == 0)
            def _():
                low = mul3(s_ref[2], inverse)
                s_ref[2] = low
                s_ref[1] = s_ref[1] - mul3(low, low)
            return carry
        lax.fori_loop(0, 2, half, 0)
        corner = -mul3(w_ref[1], mul3(s_ref[2], w_ref[0], NN), NN)
        fac_ref[k] = jnp.concatenate([jnp.concatenate([f_ref[0], zero], 1), jnp.concatenate([s_ref[2], f_ref[1]], 1)], 0)
        inv = jnp.concatenate([jnp.concatenate([w_ref[0], zero], 1), jnp.concatenate([corner, w_ref[1]], 1)], 0)
        ih, il = split(inv)
        ih_ref[k] = ih
        il_ref[k] = il
        for at in range(panels - 1):
            @pl.when(k == at)
            def _(at=at):
                rest = panels - 1 - at
                below = a_ref[at * panels + at + 1:(at + 1) * panels].reshape(rest * BS, BS)
                xh, xl = split(dot3(*split(below), ih, il))
                lh_ref[at, at + 1:] = xh.reshape(rest, BS, BS)
                ll_ref[at, at + 1:] = xl.reshape(rest, BS, BS)
                for j in range(at + 1, panels):
                    o = (j - at - 1) * BS
                    old = a_ref[j * panels + j:(j + 1) * panels]
                    upd = dot3(xh[o:], xl[o:], xh[o:o + BS], xl[o:o + BS])
                    a_ref[j * panels + j:(j + 1) * panels] = old - upd.reshape(panels - j, BS, BS)
        return carry
    lax.fori_loop(0, panels, panel, 0)

def chol(top, panels=6):
    f32, bf = jnp.float32, jnp.bfloat16
    return pl.pallas_call(
        lambda *refs: chol_kernel(panels, *refs),
        out_shape=[jax.ShapeDtypeStruct((panels, panels, BS, BS), bf)] * 2 + [jax.ShapeDtypeStruct((panels, BS, BS), bf)] * 2 + [jax.ShapeDtypeStruct((panels, BS, BS), f32)],
        scratch_shapes=[pltpu.VMEM((panels * panels, BS, BS), f32), pltpu.VMEM((3, LEAF, LEAF), f32), pltpu.VMEM((2, LEAF, LEAF), f32), pltpu.VMEM((2, LEAF, LEAF), f32)],
        compiler_params=pltpu.CompilerParams(vmem_limit_bytes=56 * 2**20),
        name="top",
    )(top)

HALF_ROWS = 4
N_ROW = 8
N_COL = 16
STRIP = BS // N_COL
CHUNK = BS // N_ROW
ROW_SLOTS = 6
COL_SLOTS = 3
ROW_TILE = 2


def solve_rows(x_ref, f_ref, h_ref, l_ref, rows, lh_ref, ll_ref, ih_ref, il_ref):
    for k in range(PANELS):
        acc = x_ref[k, :rows]
        for m in range(k):
            acc = acc - dot3(h_ref[m, :rows], l_ref[m, :rows], lh_ref[m, k], ll_ref[m, k])
        out = dot3(*split(acc), ih_ref[k], il_ref[k])
        hi, lo = split(out)
        h_ref[k, :rows] = hi
        l_ref[k, :rows] = lo
        if f_ref is not None:
            f_ref[k, :rows] = out


def rows_kernel(place_ref, row_ref, *refs):
    pieces = refs[:N_ROW]
    lh_ref, ll_ref, ih_ref, il_ref, fac_ref, front_ref, out_ref, x_ref, f_ref, rh_ref, rl_ref, ch_ref, cl_ref = refs[N_ROW:]
    r, c = place_ref[0], place_ref[1]
    step = pl.program_id(0)
    blank = jnp.zeros((BS, BS), jnp.bfloat16)

    @pl.when(step == 0)
    def _():
        for m in range(N_ROW):
            at = (r ^ m) * CHUNK
            for k in range(PANELS):
                for s in range(COL_SLOTS):
                    x_ref[k, pl.ds(pl.multiple_of(s * BS + at, CHUNK), CHUNK)] = pieces[m][k, s]
        solve_rows(x_ref, None, ch_ref, cl_ref, COL_SLOTS * BS, lh_ref, ll_ref, ih_ref, il_ref)
        for k in range(PANELS):
            @pl.when(k >= c)
            def _(k=k):
                ch_ref[k, :BS] = blank
                cl_ref[k, :BS] = blank

    @pl.when(step > 0)
    def _():
        rows = ROW_TILE * BS
        for k in range(PANELS):
            for s in range(ROW_TILE):
                x_ref[k, s * BS:(s + 1) * BS] = row_ref[:, k, s].reshape(BS, BS)
        solve_rows(x_ref, f_ref, rh_ref, rl_ref, rows, lh_ref, ll_ref, ih_ref, il_ref)

        @pl.when(step == 1)
        def _():
            for k in range(PANELS):
                @pl.when(k >= r)
                def _(k=k):
                    rh_ref[k, :BS] = blank
                    rl_ref[k, :BS] = blank
        acc = front_ref[...]
        for k in range(PANELS):
            acc = acc - dot3(rh_ref[k], rl_ref[k], ch_ref[k], cl_ref[k])
        out_ref[...] = acc

        @pl.when(c < PANELS)
        def _():
            for s in range(ROW_TILE):
                level = ((step - 1) * ROW_TILE + s) * N_ROW + r

                @pl.when(level > c)
                def _(s=s):
                    out_ref[s * BS:(s + 1) * BS, :BS] = f_ref[c, s * BS:(s + 1) * BS]

                @pl.when(level == c)
                def _(s=s):
                    out_ref[s * BS:(s + 1) * BS, :BS] = fac_ref[c]


def finish(place, row_panel, pieces, lh, ll, ih, il, fac, front):
    f32, bf = jnp.float32, jnp.bfloat16
    tiles = ROW_SLOTS // ROW_TILE
    whole = pl.BlockSpec(memory_space=pltpu.VMEM)
    tile_at = lambda g: jnp.maximum(g - 1, 0)
    rows, cols = ROW_TILE * BS, COL_SLOTS * BS
    front_spec = pl.BlockSpec((rows, cols), lambda g: (tile_at(g), 0))
    return pl.pallas_call(
        rows_kernel,
        grid=(tiles + 1,),
        in_specs=[
            pl.BlockSpec(memory_space=pltpu.SMEM),
            pl.BlockSpec((N_COL, PANELS, ROW_TILE, STRIP, BS), lambda g: (0, 0, tile_at(g), 0, 0)),
        ]
        + [whole] * N_ROW
        + [whole] * 5
        + [front_spec],
        out_specs=front_spec,
        out_shape=jax.ShapeDtypeStruct(front.shape, f32),
        scratch_shapes=[
            pltpu.VMEM((PANELS, cols, BS), f32),
            pltpu.VMEM((PANELS, rows, BS), f32),
            pltpu.VMEM((PANELS, rows, BS), bf),
            pltpu.VMEM((PANELS, rows, BS), bf),
            pltpu.VMEM((PANELS, cols, BS), bf),
            pltpu.VMEM((PANELS, cols, BS), bf),
        ],
        compiler_params=pltpu.CompilerParams(vmem_limit_bytes=60 * 2**20),
        name="finish",
    )(place, row_panel, *pieces, lh, ll, ih, il, fac, front)


def device(r, c):
    return r * N_COL + c


def permute(x, pairs):
    return lax.ppermute(x, ("row", "col"), pairs)


def swap_rows(x, apart, cols):
    return permute(x, [(device(r, c), device(r ^ apart, c)) for r in range(N_ROW) for c in cols])


def on_device(front_orig, pivot_shift, child_update, child_map):
    r = lax.axis_index("row")
    c = lax.axis_index("col")
    first = r < HALF_ROWS
    owner = c < PANELS

    child = child_update.reshape(4, 2, BS, 2, BS)
    outgoing = jnp.where(first, child[:, 1], child[:, 0])
    staying = jnp.where(first, child[:, 0], child[:, 1])
    lead, tail = outgoing[:, :, 0], outgoing[:, :, 1]
    lead_in = swap_rows(lead, HALF_ROWS, range(PANELS))
    lead_late = swap_rows(lead, HALF_ROWS, range(PANELS, N_COL))
    tail_in = swap_rows(tail, HALF_ROWS, range(N_COL))

    entry = jnp.arange(child_map.shape[1], dtype=jnp.int32)
    want_row = jnp.arange(4, dtype=jnp.int32) * N_ROW + r
    want_col = jnp.arange(2, dtype=jnp.int32) * N_COL + c

    def lookup(wanted):
        hit = wanted[None, :, None] == entry[None, None, :]
        return jnp.sum(jnp.where(hit, child_map[:, None, :], 0), axis=2)

    row_at = lookup(want_row) // N_ROW
    col_at = lookup(want_col) // N_COL

    def put_rows(part, h, slot):
        total = jnp.zeros(part.shape[1:], jnp.float32)
        for q in range(4):
            if slot % 2 == q % 2 and 0 <= slot - q <= 2:
                total = jnp.where(row_at[h, q] == slot, part[q], total)
        return total

    shift = lax.dynamic_index_in_dim(pivot_shift.reshape(ROW_SLOTS, N_ROW, BS), r, axis=1, keepdims=False)
    eye = lax.broadcasted_iota(jnp.int32, (BS, BS), 0) == lax.broadcasted_iota(jnp.int32, (BS, BS), 1)

    def with_shift(tile, p, s):
        on_diagonal = eye & (p * N_ROW + r == s * N_COL + c)
        return tile + jnp.where(on_diagonal, shift[p][:, None], 0.0)

    def front_tile(p, s):
        return with_shift(front_orig[p * BS:(p + 1) * BS, s * BS:(s + 1) * BS], p, s)

    def child_part(h, side, arrived):
        return jnp.where(first == (h == 0), side, arrived)

    column = []
    for p in range(ROW_SLOTS):
        tile = front_tile(p, 0)
        for h in range(2):
            part = child_part(h, staying[:, :, 0], lead_in)
            tile = tile + jnp.where(col_at[h, 0] == 0, put_rows(part, h, p), 0.0)
        column.append(tile)

    strips = lax.all_to_all(column[0].reshape(N_COL, STRIP, BS), "col", 0, 0)[:PANELS]
    near = [strips] + [
        permute(strips, [(device(i, k), device(i ^ m, k)) for i in range(PANELS) for k in range(N_COL)])
        for m in range(1, N_ROW)
    ]
    near = jnp.stack(near)
    packed = jnp.concatenate(
        [lax.dynamic_index_in_dim(near, r ^ i, 0, keepdims=False)[: i + 1] for i in range(PANELS)], axis=0
    )
    top = lax.all_gather(packed, "col")

    column = jnp.stack(column)
    row_part = column[1:].reshape(ROW_SLOTS - 1, N_COL, STRIP, BS).transpose(1, 0, 2, 3)
    row_part = row_part.reshape(N_COL, (ROW_SLOTS - 1) * STRIP, BS)
    col_part = column.reshape(COL_SLOTS, 2, N_ROW, CHUNK, BS).transpose(1, 2, 0, 3, 4)
    col_part = col_part.reshape(N_COL, COL_SLOTS * CHUNK, BS)
    cut = (ROW_SLOTS - 1) * STRIP
    dealt = lax.all_to_all(jnp.concatenate([row_part, col_part], axis=1), "col", 0, 0)[:PANELS]
    row_piece = jnp.concatenate(
        [strips[:, None], dealt[:, :cut].reshape(PANELS, ROW_SLOTS - 1, STRIP, BS)], axis=1
    )
    row_panel = lax.all_gather(row_piece, "col")
    col_piece = dealt[:, cut:].reshape(PANELS, COL_SLOTS, CHUNK, BS)
    col_piece = permute(
        col_piece,
        [
            (device(i, h * N_ROW + j), device(j, h * N_ROW + i))
            for i in range(N_ROW)
            for j in range(N_ROW)
            for h in range(2)
        ],
    )
    pieces = [col_piece] + [swap_rows(col_piece, m, range(N_COL)) for m in range(1, N_ROW)]

    factored = chol(top)

    lead_all = jnp.where(owner, lead_in, lead_late)
    tiles = []
    for p in range(ROW_SLOTS):
        line = []
        for s in range(COL_SLOTS):
            tile = front_tile(p, s)
            for h in range(2):
                here = child_part(h, staying[:, :, 0], lead_all)
                there = child_part(h, staying[:, :, 1], tail_in)
                a = put_rows(here, h, p) if s < 2 else None
                b = put_rows(there, h, p) if s > 0 else None
                extra = jnp.zeros_like(tile)
                if a is not None:
                    extra = jnp.where(col_at[h, 0] == s, a, extra)
                if b is not None:
                    extra = jnp.where(col_at[h, 1] == s, b, extra)
                tile = tile + extra
            line.append(tile)
        tiles.append(jnp.concatenate(line, axis=1))
    front = jnp.concatenate(tiles, axis=0)
    place = jnp.stack([r, c]).astype(jnp.int32)
    return finish(place, row_panel, pieces, *factored, front)


def solution(mesh):
    in_specs = (P("row", "col"), P(), P("row", "col"), P())
    out_specs = P("row", "col")
    return jax.shard_map(
        on_device, mesh=mesh, in_specs=in_specs, out_specs=out_specs, check_vma=False
    )
```

```python
import jax
import jax.numpy as jnp
from jax import lax
from jax.experimental import pallas as pl
from jax.experimental.pallas import tpu as pltpu
from jax.sharding import PartitionSpec as P

PANELS = 6
BS=256
NT = (((1,), (1,)), ((), ()))
NN = (((1,), (0,)), ((), ()))

def split(x):
    hi = x.astype(jnp.bfloat16)
    return hi, (x - hi.astype(jnp.float32)).astype(jnp.bfloat16)

def dot(a, b, dims=NT):
    return lax.dot_general(a, b, dims, preferred_element_type=jnp.float32)

def dot3(ah, al, bh, bl, dims=NT):
    return dot(ah, bh, dims) + (dot(ah, bl, dims) + dot(al, bh, dims))

def mul3(a, b, dims=NT):
    return dot3(*split(a), *split(b), dims)

def leaf(sym):
    n = sym.shape[0]
    groups = n // 8
    lane = lax.broadcasted_iota(jnp.int32, (8, n), 1)
    sub = lax.broadcasted_iota(jnp.int32, (8, n), 0)
    across = lambda v, j: jnp.broadcast_to(v[:, j:j + 1], (8, n))
    down = lambda v, s: jnp.broadcast_to(v[s:s + 1, :], (8, n))
    rows = [sym[8 * h:8 * h + 8] for h in range(groups)]
    right = [jnp.where(lane == sub + 8 * h, 1.0, 0.0) for h in range(groups)]
    upper, inverse = [], []
    for g in range(groups):
        cols = [across(rows[g], 8 * g + t) for t in range(8)]
        a = {(s, t): down(cols[t], s) for t in range(8) for s in range(t, 8)}
        u = [down(rows[g], t) for t in range(8)]
        w = [down(right[g], t) for t in range(8)]
        later = range(g + 1, groups)
        x = {h: [across(rows[h], 8 * g + t) for t in range(8)] for h in later}
        for t in range(8):
            r = lax.rsqrt(a[t, t])
            for s in range(t + 1, 8):
                a[s, t] = a[s, t] * r
            u[t] = u[t] * r
            w[t] = w[t] * r
            for h in later:
                x[h][t] = x[h][t] * r
            for s in range(t + 1, 8):
                for v in range(t + 1, s + 1):
                    a[s, v] = a[s, v] - a[s, t] * a[v, t]
                u[s] = u[s] - a[s, t] * u[t]
                w[s] = w[s] - a[s, t] * w[t]
                for h in later:
                    x[h][s] = x[h][s] - a[s, t] * x[h][t]
        for h in later:
            for t in range(8):
                rows[h] = rows[h] - x[h][t] * u[t]
                right[h] = right[h] - x[h][t] * w[t]
        ug, wg = u[0], w[0]
        for t in range(1, 8):
            ug = jnp.where(sub == t, u[t], ug)
            wg = jnp.where(sub == t, w[t], wg)
        upper.append(jnp.where(lane >= sub + 8 * g, ug, 0.0))
        inverse.append(wg)
    return jnp.concatenate(upper, axis=0).T, jnp.concatenate(inverse, axis=0)

def symmetric(d):
    n = d.shape[0]
    below = lax.broadcasted_iota(jnp.int32, (n, n), 0) >= lax.broadcasted_iota(jnp.int32, (n, n), 1)
    return jnp.where(below, d, d.T)

LEAF = 128


def top_kernel(first, last, in_ref, *refs):
    lows, refs = refs[:2 * (min(last, PANELS - 1) - first)], refs[2 * (min(last, PANELS - 1) - first):]
    ih_ref, il_ref, fac_ref, refs = refs[0], refs[1], refs[2], refs[3:]
    if last < PANELS:
        on_ref, refs = refs[0], refs[1:]
    a_ref, s_ref, f_ref, w_ref = refs
    if first == 0:
        e = 0
        for i in range(PANELS):
            for k in range(i + 1):
                a_ref[k * PANELS + i] = in_ref[:, e].reshape(BS, BS)
                e += 1
    else:
        e = 0
        for k in range(first, PANELS):
            a_ref[k * PANELS + k:(k + 1) * PANELS] = in_ref[e:e + PANELS - k]
            e += PANELS - k
    zero = jnp.zeros((LEAF, LEAF), jnp.float32)

    def panel(k, carry):
        d = a_ref[k * PANELS + k]
        s_ref[0] = d[:LEAF, :LEAF]
        s_ref[1] = d[LEAF:, LEAF:]
        s_ref[2] = d[LEAF:, :LEAF]

        def half(h, carry):
            factor, inverse = leaf(symmetric(s_ref[h]))
            f_ref[h] = factor
            w_ref[h] = inverse

            @pl.when(h == 0)
            def _():
                low = mul3(s_ref[2], inverse)
                s_ref[2] = low
                s_ref[1] = s_ref[1] - mul3(low, low)
            return carry
        lax.fori_loop(0, 2, half, 0)
        corner = -mul3(w_ref[1], mul3(s_ref[2], w_ref[0], NN), NN)
        fac_ref[k - first] = jnp.concatenate(
            [jnp.concatenate([f_ref[0], zero], 1), jnp.concatenate([s_ref[2], f_ref[1]], 1)], 0
        )
        inv = jnp.concatenate([jnp.concatenate([w_ref[0], zero], 1), jnp.concatenate([corner, w_ref[1]], 1)], 0)
        ih, il = split(inv)
        ih_ref[k - first] = ih
        il_ref[k - first] = il
        for at in range(first, min(last, PANELS - 1)):
            @pl.when(k == at)
            def _(at=at):
                rest = PANELS - 1 - at
                below = a_ref[at * PANELS + at + 1:(at + 1) * PANELS].reshape(rest * BS, BS)
                xh, xl = split(dot3(*split(below), ih, il))
                lows[2 * (at - first)][...] = xh.reshape(rest, BS, BS)
                lows[2 * (at - first) + 1][...] = xl.reshape(rest, BS, BS)
                for j in range(at + 1, PANELS):
                    o = (j - at - 1) * BS
                    old = a_ref[j * PANELS + j:(j + 1) * PANELS]
                    upd = dot3(xh[o:], xl[o:], xh[o:o + BS], xl[o:o + BS])
                    a_ref[j * PANELS + j:(j + 1) * PANELS] = old - upd.reshape(PANELS - j, BS, BS)
        return carry
    lax.fori_loop(first, last, panel, 0)
    if last < PANELS:
        e = 0
        for k in range(last, PANELS):
            on_ref[e:e + PANELS - k] = a_ref[k * PANELS + k:(k + 1) * PANELS]
            e += PANELS - k


def top_part(first, last, blocks):
    f32, bf = jnp.float32, jnp.bfloat16
    n = last - first
    shapes = []
    for at in range(first, min(last, PANELS - 1)):
        shapes += [jax.ShapeDtypeStruct((PANELS - 1 - at, BS, BS), bf)] * 2
    low_count = len(shapes)
    shapes += [jax.ShapeDtypeStruct((n, BS, BS), bf)] * 2 + [jax.ShapeDtypeStruct((n, BS, BS), f32)]
    left = PANELS - last
    if left:
        shapes.append(jax.ShapeDtypeStruct((left * (left + 1) // 2, BS, BS), f32))
    out = pl.pallas_call(
        lambda *refs: top_kernel(first, last, *refs),
        out_shape=shapes,
        scratch_shapes=[
            pltpu.VMEM((PANELS * PANELS, BS, BS), f32),
            pltpu.VMEM((3, LEAF, LEAF), f32),
            pltpu.VMEM((2, LEAF, LEAF), f32),
            pltpu.VMEM((2, LEAF, LEAF), f32),
        ],
        compiler_params=pltpu.CompilerParams(vmem_limit_bytes=40 * 2**20),
        cost_estimate=pl.CostEstimate(flops=n * 11 * 10**9, bytes_accessed=n * 40 * 10**6, transcendentals=n * BS),
        name="top" + str(first),
    )(blocks)
    return out[:low_count], out[low_count:low_count + 3], out[-1] if left else None

HALF_ROWS = 4
N_ROW = 8
N_COL = 16
STRIP = BS // N_COL
ROW_SLOTS = 6
COL_SLOTS = 3
CHILD_SLOTS = 4
ROW_TILE = 2


CUTS = (0, 2, 4, 6)
LOWS = PANELS - 1
PARTS = len(CUTS) - 1


def part_of(k):
    i = max(j for j in range(PARTS) if CUTS[j] <= k)
    return i, k - CUTS[i]


def solve_rows(x_ref, f_ref, h_ref, l_ref, rows, lows, invs):
    for k in range(PANELS):
        acc = x_ref[k, :rows]
        for m in range(k):
            acc = acc - dot3(h_ref[m], l_ref[m], lows[2 * m][k - m - 1], lows[2 * m + 1][k - m - 1])
        i, o = part_of(k)
        out = dot3(*split(acc), invs[3 * i][o], invs[3 * i + 1][o])
        hi, lo = split(out)
        h_ref[k] = hi
        l_ref[k] = lo
        if f_ref is not None:
            f_ref[k] = out


def rows_kernel(place_ref, row_at_ref, col_at_ref, row_ref, *refs):
    piece_ref, refs = refs[0], refs[1:]
    lows, refs = refs[:2 * LOWS], refs[2 * LOWS:]
    invs, refs = refs[:3 * PARTS], refs[3 * PARTS:]
    shift_ref, child_ref, near_ref, rest_ref, late_ref, tail_ref, front_ref, out_ref = refs[:8]
    x_ref, f_ref, rh_ref, rl_ref, ch_ref, cl_ref = refs[8:]
    r, c = place_ref[0], place_ref[1]
    side = r // HALF_ROWS
    step = pl.program_id(0)
    blank = jnp.zeros((BS, BS), jnp.bfloat16)

    @pl.when(step == 0)
    def _():
        part = BS // N_ROW
        for i in range(N_ROW):
            x, y = (i + c) % HALF_ROWS, (i // HALF_ROWS) ^ side
            for k in range(PANELS):
                for s in range(COL_SLOTS):
                    at = s * BS + i * part
                    x_ref[k, at:at + part] = piece_ref[x, y, k, s]
        solve_rows(x_ref, None, ch_ref, cl_ref, COL_SLOTS * BS, lows, invs)
        for k in range(PANELS):
            @pl.when(k >= c)
            def _(k=k):
                ch_ref[k, :BS] = blank
                cl_ref[k, :BS] = blank

    @pl.when(step > 0)
    def _():
        rows = ROW_TILE * BS
        for k in range(PANELS):
            for s in range(ROW_TILE):
                x_ref[k, s * BS:(s + 1) * BS] = row_ref[:, k, s].reshape(BS, BS)
        solve_rows(x_ref, f_ref, rh_ref, rl_ref, rows, lows, invs)

        @pl.when(step == 1)
        def _():
            for k in range(PANELS):
                @pl.when(k >= r)
                def _(k=k):
                    rh_ref[k, :BS] = blank
                    rl_ref[k, :BS] = blank
        acc = front_ref[...]
        for k in range(PANELS):
            acc = acc - dot3(rh_ref[k], rl_ref[k], ch_ref[k], cl_ref[k])
        out_ref[...] = acc

        eye = lax.broadcasted_iota(jnp.int32, (BS, BS), 0) == lax.broadcasted_iota(jnp.int32, (BS, BS), 1)
        for s in range(ROW_TILE):
            p = (step - 1) * ROW_TILE + s
            here = slice(s * BS, (s + 1) * BS)
            for t in range(COL_SLOTS):
                there = slice(t * BS, (t + 1) * BS)

                @pl.when(p * N_ROW + r == t * N_COL + c)
                def _(p=p, here=here, there=there):
                    out_ref[here, there] += jnp.where(eye, shift_ref[pl.ds(p * N_ROW + r, 1), :], 0.0)
                for h in range(2):
                    for q in (s, s + 2):
                        for u in (0, 1):
                            if not 0 <= t - u <= 1:
                                continue
                            hit = (row_at_ref[h * CHILD_SLOTS + q] == p) & (col_at_ref[h * 2 + u] == t)

                            @pl.when(hit & (side == h))
                            def _(here=here, there=there, q=q, u=u):
                                out_ref[here, there] += child_ref[q, side, :, u * BS:(u + 1) * BS]

                            @pl.when(hit & (side != h))
                            def _(here=here, there=there, q=q, u=u):
                                if u == 1:
                                    arrived = tail_ref[q]
                                else:
                                    arrived = late_ref[q] + (near_ref[0] if q == 0 else rest_ref[q - 1])
                                out_ref[here, there] += arrived
            level = p * N_ROW + r

            @pl.when((c < PANELS) & (level > c))
            def _(here=here):
                out_ref[here, :BS] = f_ref[c, here]

            for k in range(PANELS):
                @pl.when((c == k) & (level == k))
                def _(here=here, k=k):
                    i, o = part_of(k)
                    out_ref[here, :BS] = invs[3 * i + 2][o]


def finish(place, row_at, col_at, row_panel, col_panel, lows, invs, shift, child, near, rest, late, tail, front):
    f32, bf = jnp.float32, jnp.bfloat16
    tiles = ROW_SLOTS // ROW_TILE
    whole = pl.BlockSpec(memory_space=pltpu.VMEM)
    smem = pl.BlockSpec(memory_space=pltpu.SMEM)
    tile_at = lambda g: jnp.maximum(g - 1, 0)
    rows, cols = ROW_TILE * BS, COL_SLOTS * BS
    front_spec = pl.BlockSpec((rows, cols), lambda g: (tile_at(g), 0))
    return pl.pallas_call(
        rows_kernel,
        grid=(tiles + 1,),
        in_specs=[smem] * 3
        + [pl.BlockSpec((N_COL, PANELS, ROW_TILE, STRIP, BS), lambda g: (0, 0, tile_at(g), 0, 0))]
        + [whole] * (1 + 2 * LOWS + 3 * PARTS + 6)
        + [front_spec],
        out_specs=front_spec,
        out_shape=jax.ShapeDtypeStruct(front.shape, f32),
        scratch_shapes=[
            pltpu.VMEM((PANELS, cols, BS), f32),
            pltpu.VMEM((PANELS, rows, BS), f32),
            pltpu.VMEM((PANELS, rows, BS), bf),
            pltpu.VMEM((PANELS, rows, BS), bf),
            pltpu.VMEM((PANELS, cols, BS), bf),
            pltpu.VMEM((PANELS, cols, BS), bf),
        ],
        compiler_params=pltpu.CompilerParams(vmem_limit_bytes=60 * 2**20),
        name="finish",
    )(place, row_at, col_at, row_panel, col_panel, *lows, *invs, shift, child, near, rest, late, tail, front)


def device(r, c):
    return r * N_COL + c


def permute(x, pairs):
    return lax.ppermute(x, ("row", "col"), pairs)


def swap_rows(x, apart, cols):
    return permute(x, [(device(r, c), device(r ^ apart, c)) for r in range(N_ROW) for c in cols])


def after(x, *others):
    return lax.optimization_barrier((x, *others))[0]


def on_device(front_orig, pivot_shift, child_update, child_map):
    r = lax.axis_index("row")
    c = lax.axis_index("col")
    first = r < HALF_ROWS

    child = child_update.reshape(CHILD_SLOTS, 2, BS, 2 * BS)

    def leaving(cols):
        return jnp.where(first, child[:, 1, :, cols], child[:, 0, :, cols])

    lead = leaving(slice(0, BS))
    near_in = swap_rows(lead[:1], HALF_ROWS, range(PANELS))
    entry = jnp.arange(child_map.shape[1], dtype=jnp.int32)
    want_row = jnp.arange(CHILD_SLOTS, dtype=jnp.int32) * N_ROW + r
    want_col = jnp.arange(2, dtype=jnp.int32) * N_COL + c

    def lookup(wanted):
        hit = wanted[None, :, None] == entry[None, None, :]
        return jnp.sum(jnp.where(hit, child_map[:, None, :], 0), axis=2)

    row_at = lookup(want_row) // N_ROW
    col_at = lookup(want_col) // N_COL

    staying = jnp.where(first, child[:, 0, :, :BS], child[:, 1, :, :BS])
    own = lax.dynamic_index_in_dim(pivot_shift.reshape(ROW_SLOTS, N_ROW, BS), r, axis=1, keepdims=False)
    eye = lax.broadcasted_iota(jnp.int32, (BS, BS), 0) == lax.broadcasted_iota(jnp.int32, (BS, BS), 1)

    def raw_tile(p):
        tile = front_orig[p * BS:(p + 1) * BS, :BS]
        if p == 0:
            tile = tile + jnp.where(eye & (r == c), own[0][:, None], 0.0)
        for h in range(2):
            for q in range(p % 2, CHILD_SLOTS, 2):
                if 0 <= p - q <= 2:
                    arrived = near_in[0] if q == 0 else rest_in[q - 1]
                    part = jnp.where(first == (h == 0), staying[q], arrived)
                    hit = (col_at[h, 0] == 0) & (row_at[h, q] == p)
                    tile = tile + jnp.where(hit, part, 0.0)
        return tile.reshape(N_COL, STRIP, BS)

    def row_gather(x, *groups):
        n = len(groups[0])
        groups = None if n == N_ROW else [list(g) for g in groups]
        return lax.all_to_all(jnp.broadcast_to(x, (n, *x.shape)), "row", 0, 0, axis_index_groups=groups)

    strips = lax.all_to_all(raw_tile(0), "col", 0, 0)[:PANELS]
    rest_in = swap_rows(after(lead[1:], strips), HALF_ROWS, range(PANELS))
    near = row_gather(strips, range(N_ROW))
    packed = jnp.concatenate([near[i, : i + 1] for i in range(PANELS)], axis=0)
    top = lax.all_gather(packed, "col")

    column = jnp.stack([raw_tile(p) for p in range(1, ROW_SLOTS)], axis=1)
    dealt = lax.all_to_all(after(column, packed), "col", 0, 0)[:PANELS]
    dealt = jnp.concatenate([strips[:, None], dealt], axis=1)

    lows0, invs0, blocks0 = top_part(CUTS[0], CUTS[1], top)
    lows1, invs1, blocks1 = top_part(CUTS[1], CUTS[2], blocks0)
    lows2, invs2, _ = top_part(CUTS[2], CUTS[3], blocks1)
    lows, invs = lows0 + lows1 + lows2, invs0 + invs1 + invs2

    even, odd = dealt[:, 0::2], dealt[:, 1::2]
    is_odd = c % 2 == 1
    upper = c >= N_ROW

    def turned(flip, far):
        pairs = []
        for i in range(N_ROW):
            for j in range(N_COL):
                to = (j // N_ROW) ^ far
                to = to * HALF_ROWS + (i + j % N_ROW // 2) % HALF_ROWS
                pairs.append((device(i, j), device(to, (j % 2 ^ flip) * N_ROW + i)))
        return permute(jnp.where(is_odd != (flip == 1), odd, even), pairs)

    pair = []
    for far in (0, 1):
        straight, crossed = after(turned(0, far), blocks0), after(turned(1, far), blocks0)
        pair.append(
            jnp.concatenate([jnp.where(upper, crossed, straight), jnp.where(upper, straight, crossed)], axis=2)
        )
    pair = jnp.stack(pair)
    col_panel = row_gather(pair, range(HALF_ROWS), range(HALF_ROWS, N_ROW))

    row_panel = lax.all_gather(after(dealt, top), "col")

    lead_late = swap_rows(after(lead, blocks0), HALF_ROWS, range(PANELS, N_COL))
    tail_in = swap_rows(after(leaving(slice(BS, 2 * BS)), blocks0), HALF_ROWS, range(N_COL))

    place = jnp.stack([r, c]).astype(jnp.int32)
    return finish(
        place, row_at.reshape(-1), col_at.reshape(-1), row_panel, col_panel, lows, invs,
        pivot_shift.reshape(-1, BS), child, near_in, rest_in, lead_late, tail_in, front_orig,
    )


def solution(mesh):
    in_specs = (P("row", "col"), P(), P("row", "col"), P())
    out_specs = P("row", "col")
    return jax.shard_map(
        on_device, mesh=mesh, in_specs=in_specs, out_specs=out_specs, check_vma=False
    )
```

```python
import jax
import jax.numpy as jnp
from jax import lax
from jax.experimental import pallas as pl
from jax.experimental.pallas import tpu as pltpu
from jax.sharding import PartitionSpec as P

PANELS = 6
BS=256
NT = (((1,), (1,)), ((), ()))
NN = (((1,), (0,)), ((), ()))

def split(x):
    hi = x.astype(jnp.bfloat16)
    return hi, (x - hi.astype(jnp.float32)).astype(jnp.bfloat16)

def dot(a, b, dims=NT):
    return lax.dot_general(a, b, dims, preferred_element_type=jnp.float32)

def dot3(ah, al, bh, bl, dims=NT):
    return dot(ah, bh, dims) + (dot(ah, bl, dims) + dot(al, bh, dims))

def mul3(a, b, dims=NT):
    return dot3(*split(a), *split(b), dims)

def leaf(sym):
    n = sym.shape[0]
    groups = n // 8
    lane = lax.broadcasted_iota(jnp.int32, (8, n), 1)
    sub = lax.broadcasted_iota(jnp.int32, (8, n), 0)
    across = lambda v, j: jnp.broadcast_to(v[:, j:j + 1], (8, n))
    down = lambda v, s: jnp.broadcast_to(v[s:s + 1, :], (8, n))
    rows = [sym[8 * h:8 * h + 8] for h in range(groups)]
    right = [jnp.where(lane == sub + 8 * h, 1.0, 0.0) for h in range(groups)]
    upper, inverse = [], []
    for g in range(groups):
        cols = [across(rows[g], 8 * g + t) for t in range(8)]
        a = {(s, t): down(cols[t], s) for t in range(8) for s in range(t, 8)}
        u = [down(rows[g], t) for t in range(8)]
        w = [down(right[g], t) for t in range(8)]
        later = range(g + 1, groups)
        x = {h: [across(rows[h], 8 * g + t) for t in range(8)] for h in later}
        for t in range(8):
            r = lax.rsqrt(a[t, t])
            for s in range(t + 1, 8):
                a[s, t] = a[s, t] * r
            u[t] = u[t] * r
            w[t] = w[t] * r
            for h in later:
                x[h][t] = x[h][t] * r
            for s in range(t + 1, 8):
                for v in range(t + 1, s + 1):
                    a[s, v] = a[s, v] - a[s, t] * a[v, t]
                u[s] = u[s] - a[s, t] * u[t]
                w[s] = w[s] - a[s, t] * w[t]
                for h in later:
                    x[h][s] = x[h][s] - a[s, t] * x[h][t]
        for h in later:
            for t in range(8):
                rows[h] = rows[h] - x[h][t] * u[t]
                right[h] = right[h] - x[h][t] * w[t]
        ug, wg = u[0], w[0]
        for t in range(1, 8):
            ug = jnp.where(sub == t, u[t], ug)
            wg = jnp.where(sub == t, w[t], wg)
        upper.append(jnp.where(lane >= sub + 8 * g, ug, 0.0))
        inverse.append(wg)
    return jnp.concatenate(upper, axis=0).T, jnp.concatenate(inverse, axis=0)

def symmetric(d):
    n = d.shape[0]
    below = lax.broadcasted_iota(jnp.int32, (n, n), 0) >= lax.broadcasted_iota(jnp.int32, (n, n), 1)
    return jnp.where(below, d, d.T)

LEAF = 128


def top_kernel(first, last, in_ref, *refs):
    lows, refs = refs[:2 * (min(last, PANELS - 1) - first)], refs[2 * (min(last, PANELS - 1) - first):]
    ih_ref, il_ref, fac_ref, refs = refs[0], refs[1], refs[2], refs[3:]
    if last < PANELS:
        on_ref, refs = refs[0], refs[1:]
    a_ref, s_ref, f_ref, w_ref = refs
    if first == 0:
        e = 0
        for i in range(PANELS):
            for k in range(i + 1):
                a_ref[k * PANELS + i] = in_ref[:, e].reshape(BS, BS)
                e += 1
    else:
        e = 0
        for k in range(first, PANELS):
            a_ref[k * PANELS + k:(k + 1) * PANELS] = in_ref[e:e + PANELS - k]
            e += PANELS - k
    zero = jnp.zeros((LEAF, LEAF), jnp.float32)

    def panel(k, carry):
        d = a_ref[k * PANELS + k]
        s_ref[0] = d[:LEAF, :LEAF]
        s_ref[1] = d[LEAF:, LEAF:]
        s_ref[2] = d[LEAF:, :LEAF]

        def half(h, carry):
            factor, inverse = leaf(symmetric(s_ref[h]))
            f_ref[h] = factor
            w_ref[h] = inverse

            @pl.when(h == 0)
            def _():
                low = mul3(s_ref[2], inverse)
                s_ref[2] = low
                s_ref[1] = s_ref[1] - mul3(low, low)
            return carry
        lax.fori_loop(0, 2, half, 0)
        corner = -mul3(w_ref[1], mul3(s_ref[2], w_ref[0], NN), NN)
        fac_ref[k - first] = jnp.concatenate(
            [jnp.concatenate([f_ref[0], zero], 1), jnp.concatenate([s_ref[2], f_ref[1]], 1)], 0
        )
        inv = jnp.concatenate([jnp.concatenate([w_ref[0], zero], 1), jnp.concatenate([corner, w_ref[1]], 1)], 0)
        ih, il = split(inv)
        ih_ref[k - first] = ih
        il_ref[k - first] = il
        for at in range(first, min(last, PANELS - 1)):
            @pl.when(k == at)
            def _(at=at):
                rest = PANELS - 1 - at
                below = a_ref[at * PANELS + at + 1:(at + 1) * PANELS].reshape(rest * BS, BS)
                xh, xl = split(dot3(*split(below), ih, il))
                lows[2 * (at - first)][...] = xh.reshape(rest, BS, BS)
                lows[2 * (at - first) + 1][...] = xl.reshape(rest, BS, BS)
                for j in range(at + 1, PANELS):
                    o = (j - at - 1) * BS
                    old = a_ref[j * PANELS + j:(j + 1) * PANELS]
                    upd = dot3(xh[o:], xl[o:], xh[o:o + BS], xl[o:o + BS])
                    a_ref[j * PANELS + j:(j + 1) * PANELS] = old - upd.reshape(PANELS - j, BS, BS)
        return carry
    lax.fori_loop(first, last, panel, 0)
    if last < PANELS:
        e = 0
        for k in range(last, PANELS):
            on_ref[e:e + PANELS - k] = a_ref[k * PANELS + k:(k + 1) * PANELS]
            e += PANELS - k


def top_part(first, last, blocks):
    f32, bf = jnp.float32, jnp.bfloat16
    n = last - first
    shapes = []
    for at in range(first, min(last, PANELS - 1)):
        shapes += [jax.ShapeDtypeStruct((PANELS - 1 - at, BS, BS), bf)] * 2
    low_count = len(shapes)
    shapes += [jax.ShapeDtypeStruct((n, BS, BS), bf)] * 2 + [jax.ShapeDtypeStruct((n, BS, BS), f32)]
    left = PANELS - last
    if left:
        shapes.append(jax.ShapeDtypeStruct((left * (left + 1) // 2, BS, BS), f32))
    out = pl.pallas_call(
        lambda *refs: top_kernel(first, last, *refs),
        out_shape=shapes,
        scratch_shapes=[
            pltpu.VMEM((PANELS * PANELS, BS, BS), f32),
            pltpu.VMEM((3, LEAF, LEAF), f32),
            pltpu.VMEM((2, LEAF, LEAF), f32),
            pltpu.VMEM((2, LEAF, LEAF), f32),
        ],
        compiler_params=pltpu.CompilerParams(vmem_limit_bytes=40 * 2**20),
        cost_estimate=pl.CostEstimate(flops=n * 11 * 10**9, bytes_accessed=n * 40 * 10**6, transcendentals=n * BS),
        name="top" + str(first),
    )(blocks)
    return out[:low_count], out[low_count:low_count + 3], out[-1] if left else None

HALF_ROWS = 4
N_ROW = 8
N_COL = 16
STRIP = BS // N_COL
ROW_SLOTS = 6
COL_SLOTS = 3
CHILD_SLOTS = 4
ROW_TILE = 2


CUTS = (0, 1, 2, 4, 6)
LOWS = PANELS - 1
PARTS = len(CUTS) - 1


def part_of(k):
    i = max(j for j in range(PARTS) if CUTS[j] <= k)
    return i, k - CUTS[i]


def solve_rows(x_ref, f_ref, h_ref, l_ref, rows, lows, invs):
    for k in range(PANELS):
        acc = x_ref[k, :rows]
        for m in range(k):
            acc = acc - dot3(h_ref[m], l_ref[m], lows[2 * m][k - m - 1], lows[2 * m + 1][k - m - 1])
        i, o = part_of(k)
        out = dot3(*split(acc), invs[3 * i][o], invs[3 * i + 1][o])
        hi, lo = split(out)
        h_ref[k] = hi
        l_ref[k] = lo
        if f_ref is not None:
            f_ref[k] = out


def rows_kernel(place_ref, row_at_ref, col_at_ref, row_ref, *refs):
    piece_ref, refs = refs[0], refs[1:]
    lows, refs = refs[:2 * LOWS], refs[2 * LOWS:]
    invs, refs = refs[:3 * PARTS], refs[3 * PARTS:]
    shift_ref, child_ref, near_ref, rest_ref, late_ref, tail_ref, front_ref, out_ref = refs[:8]
    x_ref, f_ref, rh_ref, rl_ref, ch_ref, cl_ref = refs[8:]
    r, c = place_ref[0], place_ref[1]
    side = r // HALF_ROWS
    step = pl.program_id(0)
    blank = jnp.zeros((BS, BS), jnp.bfloat16)

    @pl.when(step == 0)
    def _():
        part = BS // N_ROW
        for i in range(N_ROW):
            x, y = (i + c) % HALF_ROWS, (i // HALF_ROWS) ^ side
            for k in range(PANELS):
                for s in range(COL_SLOTS):
                    at = s * BS + i * part
                    x_ref[k, at:at + part] = piece_ref[x, y, k, s]
        solve_rows(x_ref, None, ch_ref, cl_ref, COL_SLOTS * BS, lows, invs)
        for k in range(PANELS):
            @pl.when(k >= c)
            def _(k=k):
                ch_ref[k, :BS] = blank
                cl_ref[k, :BS] = blank

    @pl.when(step > 0)
    def _():
        rows = ROW_TILE * BS
        for k in range(PANELS):
            for s in range(ROW_TILE):
                x_ref[k, s * BS:(s + 1) * BS] = row_ref[:, k, s].reshape(BS, BS)
        solve_rows(x_ref, f_ref, rh_ref, rl_ref, rows, lows, invs)

        @pl.when(step == 1)
        def _():
            for k in range(PANELS):
                @pl.when(k >= r)
                def _(k=k):
                    rh_ref[k, :BS] = blank
                    rl_ref[k, :BS] = blank
        acc = front_ref[...]
        for k in range(PANELS):
            acc = acc - dot3(rh_ref[k], rl_ref[k], ch_ref[k], cl_ref[k])
        out_ref[...] = acc

        eye = lax.broadcasted_iota(jnp.int32, (BS, BS), 0) == lax.broadcasted_iota(jnp.int32, (BS, BS), 1)
        for s in range(ROW_TILE):
            p = (step - 1) * ROW_TILE + s
            here = slice(s * BS, (s + 1) * BS)
            for t in range(COL_SLOTS):
                there = slice(t * BS, (t + 1) * BS)

                @pl.when(p * N_ROW + r == t * N_COL + c)
                def _(p=p, here=here, there=there):
                    out_ref[here, there] += jnp.where(eye, shift_ref[pl.ds(p * N_ROW + r, 1), :], 0.0)
                for h in range(2):
                    for q in (s, s + 2):
                        for u in (0, 1):
                            if not 0 <= t - u <= 1:
                                continue
                            hit = (row_at_ref[h * CHILD_SLOTS + q] == p) & (col_at_ref[h * 2 + u] == t)

                            @pl.when(hit & (side == h))
                            def _(here=here, there=there, q=q, u=u):
                                out_ref[here, there] += child_ref[q, side, :, u * BS:(u + 1) * BS]

                            @pl.when(hit & (side != h))
                            def _(here=here, there=there, q=q, u=u):
                                if u == 1:
                                    arrived = tail_ref[q]
                                else:
                                    arrived = late_ref[q] + (near_ref[0] if q == 0 else rest_ref[q - 1])
                                out_ref[here, there] += arrived
            level = p * N_ROW + r

            @pl.when((c < PANELS) & (level > c))
            def _(here=here):
                out_ref[here, :BS] = f_ref[c, here]

            for k in range(PANELS):
                @pl.when((c == k) & (level == k))
                def _(here=here, k=k):
                    i, o = part_of(k)
                    out_ref[here, :BS] = invs[3 * i + 2][o]


def finish(place, row_at, col_at, row_panel, col_panel, lows, invs, shift, child, near, rest, late, tail, front):
    f32, bf = jnp.float32, jnp.bfloat16
    tiles = ROW_SLOTS // ROW_TILE
    whole = pl.BlockSpec(memory_space=pltpu.VMEM)
    smem = pl.BlockSpec(memory_space=pltpu.SMEM)
    tile_at = lambda g: jnp.maximum(g - 1, 0)
    rows, cols = ROW_TILE * BS, COL_SLOTS * BS
    front_spec = pl.BlockSpec((rows, cols), lambda g: (tile_at(g), 0))
    return pl.pallas_call(
        rows_kernel,
        grid=(tiles + 1,),
        in_specs=[smem] * 3
        + [pl.BlockSpec((N_COL, PANELS, ROW_TILE, STRIP, BS), lambda g: (0, 0, tile_at(g), 0, 0))]
        + [whole] * (1 + 2 * LOWS + 3 * PARTS + 6)
        + [front_spec],
        out_specs=front_spec,
        out_shape=jax.ShapeDtypeStruct(front.shape, f32),
        scratch_shapes=[
            pltpu.VMEM((PANELS, cols, BS), f32),
            pltpu.VMEM((PANELS, rows, BS), f32),
            pltpu.VMEM((PANELS, rows, BS), bf),
            pltpu.VMEM((PANELS, rows, BS), bf),
            pltpu.VMEM((PANELS, cols, BS), bf),
            pltpu.VMEM((PANELS, cols, BS), bf),
        ],
        compiler_params=pltpu.CompilerParams(vmem_limit_bytes=60 * 2**20),
        name="finish",
    )(place, row_at, col_at, row_panel, col_panel, *lows, *invs, shift, child, near, rest, late, tail, front)


def device(r, c):
    return r * N_COL + c


def permute(x, pairs):
    return lax.ppermute(x, ("row", "col"), pairs)


def swap_rows(x, apart, cols):
    return permute(x, [(device(r, c), device(r ^ apart, c)) for r in range(N_ROW) for c in cols])


def after(x, *others):
    return lax.optimization_barrier((x, *others))[0]


def on_device(front_orig, pivot_shift, child_update, child_map):
    r = lax.axis_index("row")
    c = lax.axis_index("col")
    first = r < HALF_ROWS

    child = child_update.reshape(CHILD_SLOTS, 2, BS, 2 * BS)

    def leaving(cols):
        return jnp.where(first, child[:, 1, :, cols], child[:, 0, :, cols])

    lead = leaving(slice(0, BS))
    near_in = swap_rows(lead[:1], HALF_ROWS, range(PANELS))
    entry = jnp.arange(child_map.shape[1], dtype=jnp.int32)
    want_row = jnp.arange(CHILD_SLOTS, dtype=jnp.int32) * N_ROW + r
    want_col = jnp.arange(2, dtype=jnp.int32) * N_COL + c

    def lookup(wanted):
        hit = wanted[None, :, None] == entry[None, None, :]
        return jnp.sum(jnp.where(hit, child_map[:, None, :], 0), axis=2)

    row_at = lookup(want_row) // N_ROW
    col_at = lookup(want_col) // N_COL

    staying = jnp.where(first, child[:, 0, :, :BS], child[:, 1, :, :BS])
    own = lax.dynamic_index_in_dim(pivot_shift.reshape(ROW_SLOTS, N_ROW, BS), r, axis=1, keepdims=False)
    eye = lax.broadcasted_iota(jnp.int32, (BS, BS), 0) == lax.broadcasted_iota(jnp.int32, (BS, BS), 1)

    def raw_tile(p):
        tile = front_orig[p * BS:(p + 1) * BS, :BS]
        if p == 0:
            tile = tile + jnp.where(eye & (r == c), own[0][:, None], 0.0)
        for h in range(2):
            for q in range(p % 2, CHILD_SLOTS, 2):
                if 0 <= p - q <= 2:
                    arrived = near_in[0] if q == 0 else rest_in[q - 1]
                    part = jnp.where(first == (h == 0), staying[q], arrived)
                    hit = (col_at[h, 0] == 0) & (row_at[h, q] == p)
                    tile = tile + jnp.where(hit, part, 0.0)
        return tile.reshape(N_COL, STRIP, BS)

    def row_gather(x, *groups):
        n = len(groups[0])
        groups = None if n == N_ROW else [list(g) for g in groups]
        return lax.all_to_all(jnp.broadcast_to(x, (n, *x.shape)), "row", 0, 0, axis_index_groups=groups)

    strips = lax.all_to_all(raw_tile(0), "col", 0, 0)[:PANELS]
    rest_in = swap_rows(after(lead[1:], strips), HALF_ROWS, range(PANELS))
    near = after(row_gather(strips, range(N_ROW)), rest_in)
    packed = jnp.concatenate([near[i, : i + 1] for i in range(PANELS)], axis=0)
    top = lax.all_gather(packed, "col")

    column = jnp.stack([raw_tile(p) for p in range(1, ROW_SLOTS)], axis=1)
    dealt = lax.all_to_all(after(column, packed), "col", 0, 0)[:PANELS]
    dealt = jnp.concatenate([strips[:, None], dealt], axis=1)

    lows, invs, blocks, done = [], [], top, []
    for i in range(PARTS):
        low, inv, blocks = top_part(CUTS[i], CUTS[i + 1], blocks)
        lows, invs = lows + list(low), invs + list(inv)
        if i < 2:
            done.append(blocks)

    even, odd = dealt[:, 0::2], dealt[:, 1::2]
    is_odd = c % 2 == 1
    upper = c >= N_ROW

    def turned(flip, far):
        pairs = []
        for i in range(N_ROW):
            for j in range(N_COL):
                to = (j // N_ROW) ^ far
                to = to * HALF_ROWS + (i + j % N_ROW // 2) % HALF_ROWS
                pairs.append((device(i, j), device(to, (j % 2 ^ flip) * N_ROW + i)))
        return permute(jnp.where(is_odd != (flip == 1), odd, even), pairs)

    pair = []
    for far in (0, 1):
        straight, crossed = after(turned(0, far), done[0]), after(turned(1, far), done[0])
        pair.append(
            jnp.concatenate([jnp.where(upper, crossed, straight), jnp.where(upper, straight, crossed)], axis=2)
        )
    pair = jnp.stack(pair)
    col_panel = row_gather(pair, range(HALF_ROWS), range(HALF_ROWS, N_ROW))

    row_panel = lax.all_gather(dealt, "col")

    lead_late = swap_rows(after(lead, done[1]), HALF_ROWS, range(PANELS, N_COL))
    tail_in = swap_rows(after(leaving(slice(BS, 2 * BS)), done[1]), HALF_ROWS, range(N_COL))

    place = jnp.stack([r, c]).astype(jnp.int32)
    return finish(
        place, row_at.reshape(-1), col_at.reshape(-1), row_panel, col_panel, lows, invs,
        pivot_shift.reshape(-1, BS), child, near_in, rest_in, lead_late, tail_in, front_orig,
    )


def solution(mesh):
    in_specs = (P("row", "col"), P(), P("row", "col"), P())
    out_specs = P("row", "col")
    return jax.shard_map(
        on_device, mesh=mesh, in_specs=in_specs, out_specs=out_specs, check_vma=False
    )
```

```python
import jax
import jax.numpy as jnp
from jax import lax
from jax.experimental import pallas as pl
from jax.experimental.pallas import tpu as pltpu
from jax.sharding import PartitionSpec as P

PANELS = 6
BS=256
NT = (((1,), (1,)), ((), ()))
NN = (((1,), (0,)), ((), ()))

def split(x):
    hi = x.astype(jnp.bfloat16)
    return hi, (x - hi.astype(jnp.float32)).astype(jnp.bfloat16)

def dot(a, b, dims=NT):
    return lax.dot_general(a, b, dims, preferred_element_type=jnp.float32)

def dot3(ah, al, bh, bl, dims=NT):
    return dot(ah, bh, dims) + (dot(ah, bl, dims) + dot(al, bh, dims))

def mul3(a, b, dims=NT):
    return dot3(*split(a), *split(b), dims)

def leaf(sym):
    n = sym.shape[0]
    groups = n // 8
    lane = lax.broadcasted_iota(jnp.int32, (8, n), 1)
    sub = lax.broadcasted_iota(jnp.int32, (8, n), 0)
    across = lambda v, j: jnp.broadcast_to(v[:, j:j + 1], (8, n))
    down = lambda v, s: jnp.broadcast_to(v[s:s + 1, :], (8, n))
    rows = [sym[8 * h:8 * h + 8] for h in range(groups)]
    right = [jnp.where(lane == sub + 8 * h, 1.0, 0.0) for h in range(groups)]
    upper, inverse = [], []
    for g in range(groups):
        cols = [across(rows[g], 8 * g + t) for t in range(8)]
        a = {(s, t): down(cols[t], s) for t in range(8) for s in range(t, 8)}
        u = [down(rows[g], t) for t in range(8)]
        w = [down(right[g], t) for t in range(8)]
        later = range(g + 1, groups)
        x = {h: [across(rows[h], 8 * g + t) for t in range(8)] for h in later}
        for t in range(8):
            r = lax.rsqrt(a[t, t])
            for s in range(t + 1, 8):
                a[s, t] = a[s, t] * r
            u[t] = u[t] * r
            w[t] = w[t] * r
            for h in later:
                x[h][t] = x[h][t] * r
            for s in range(t + 1, 8):
                for v in range(t + 1, s + 1):
                    a[s, v] = a[s, v] - a[s, t] * a[v, t]
                u[s] = u[s] - a[s, t] * u[t]
                w[s] = w[s] - a[s, t] * w[t]
                for h in later:
                    x[h][s] = x[h][s] - a[s, t] * x[h][t]
        for h in later:
            for t in range(8):
                rows[h] = rows[h] - x[h][t] * u[t]
                right[h] = right[h] - x[h][t] * w[t]
        ug, wg = u[0], w[0]
        for t in range(1, 8):
            ug = jnp.where(sub == t, u[t], ug)
            wg = jnp.where(sub == t, w[t], wg)
        upper.append(jnp.where(lane >= sub + 8 * g, ug, 0.0))
        inverse.append(wg)
    return jnp.concatenate(upper, axis=0).T, jnp.concatenate(inverse, axis=0)

def symmetric(d):
    n = d.shape[0]
    below = lax.broadcasted_iota(jnp.int32, (n, n), 0) >= lax.broadcasted_iota(jnp.int32, (n, n), 1)
    return jnp.where(below, d, d.T)

LEAF = 128


def top_kernel(first, last, in_ref, *refs):
    lows, refs = refs[:2 * (min(last, PANELS - 1) - first)], refs[2 * (min(last, PANELS - 1) - first):]
    ih_ref, il_ref, fac_ref, refs = refs[0], refs[1], refs[2], refs[3:]
    if last < PANELS:
        on_ref, refs = refs[0], refs[1:]
    a_ref, s_ref, f_ref, w_ref = refs
    if first == 0:
        e = 0
        for i in range(PANELS):
            for k in range(i + 1):
                a_ref[k * PANELS + i] = in_ref[:, e].reshape(BS, BS)
                e += 1
    else:
        e = 0
        for k in range(first, PANELS):
            a_ref[k * PANELS + k:(k + 1) * PANELS] = in_ref[e:e + PANELS - k]
            e += PANELS - k
    zero = jnp.zeros((LEAF, LEAF), jnp.float32)

    def panel(k, carry):
        d = a_ref[k * PANELS + k]
        s_ref[0] = d[:LEAF, :LEAF]
        s_ref[1] = d[LEAF:, LEAF:]
        s_ref[2] = d[LEAF:, :LEAF]

        def half(h, carry):
            factor, inverse = leaf(symmetric(s_ref[h]))
            f_ref[h] = factor
            w_ref[h] = inverse

            @pl.when(h == 0)
            def _():
                low = mul3(s_ref[2], inverse)
                s_ref[2] = low
                s_ref[1] = s_ref[1] - mul3(low, low)
            return carry
        lax.fori_loop(0, 2, half, 0)
        corner = -mul3(w_ref[1], mul3(s_ref[2], w_ref[0], NN), NN)
        fac_ref[k - first] = jnp.concatenate(
            [jnp.concatenate([f_ref[0], zero], 1), jnp.concatenate([s_ref[2], f_ref[1]], 1)], 0
        )
        inv = jnp.concatenate([jnp.concatenate([w_ref[0], zero], 1), jnp.concatenate([corner, w_ref[1]], 1)], 0)
        ih, il = split(inv)
        ih_ref[k - first] = ih
        il_ref[k - first] = il
        for at in range(first, min(last, PANELS - 1)):
            @pl.when(k == at)
            def _(at=at):
                rest = PANELS - 1 - at
                below = a_ref[at * PANELS + at + 1:(at + 1) * PANELS].reshape(rest * BS, BS)
                xh, xl = split(dot3(*split(below), ih, il))
                lows[2 * (at - first)][...] = xh.reshape(rest, BS, BS)
                lows[2 * (at - first) + 1][...] = xl.reshape(rest, BS, BS)
                for j in range(at + 1, PANELS):
                    o = (j - at - 1) * BS
                    old = a_ref[j * PANELS + j:(j + 1) * PANELS]
                    upd = dot3(xh[o:], xl[o:], xh[o:o + BS], xl[o:o + BS])
                    a_ref[j * PANELS + j:(j + 1) * PANELS] = old - upd.reshape(PANELS - j, BS, BS)
        return carry
    lax.fori_loop(first, last, panel, 0)
    if last < PANELS:
        e = 0
        for k in range(last, PANELS):
            on_ref[e:e + PANELS - k] = a_ref[k * PANELS + k:(k + 1) * PANELS]
            e += PANELS - k


def top_part(first, last, blocks):
    f32, bf = jnp.float32, jnp.bfloat16
    n = last - first
    shapes = []
    for at in range(first, min(last, PANELS - 1)):
        shapes += [jax.ShapeDtypeStruct((PANELS - 1 - at, BS, BS), bf)] * 2
    low_count = len(shapes)
    shapes += [jax.ShapeDtypeStruct((n, BS, BS), bf)] * 2 + [jax.ShapeDtypeStruct((n, BS, BS), f32)]
    left = PANELS - last
    if left:
        shapes.append(jax.ShapeDtypeStruct((left * (left + 1) // 2, BS, BS), f32))
    out = pl.pallas_call(
        lambda *refs: top_kernel(first, last, *refs),
        out_shape=shapes,
        scratch_shapes=[
            pltpu.VMEM((PANELS * PANELS, BS, BS), f32),
            pltpu.VMEM((3, LEAF, LEAF), f32),
            pltpu.VMEM((2, LEAF, LEAF), f32),
            pltpu.VMEM((2, LEAF, LEAF), f32),
        ],
        compiler_params=pltpu.CompilerParams(vmem_limit_bytes=40 * 2**20),
        cost_estimate=pl.CostEstimate(flops=n * 11 * 10**9, bytes_accessed=n * 40 * 10**6, transcendentals=n * BS),
        name="top" + str(first),
    )(blocks)
    return out[:low_count], out[low_count:low_count + 3], out[-1] if left else None

HALF_ROWS = 4
N_ROW = 8
N_COL = 16
STRIP = BS // N_COL
ROW_SLOTS = 6
COL_SLOTS = 3
CHILD_SLOTS = 4
ROW_TILE = 2


CUTS = (0, 6)
LOWS = PANELS - 1
PARTS = len(CUTS) - 1


def part_of(k):
    i = max(j for j in range(PARTS) if CUTS[j] <= k)
    return i, k - CUTS[i]


def solve_rows(x_ref, f_ref, h_ref, l_ref, rows, lows, invs):
    for k in range(PANELS):
        acc = x_ref[k, :rows]
        for m in range(k):
            acc = acc - dot3(h_ref[m], l_ref[m], lows[2 * m][k - m - 1], lows[2 * m + 1][k - m - 1])
        i, o = part_of(k)
        out = dot3(*split(acc), invs[3 * i][o], invs[3 * i + 1][o])
        hi, lo = split(out)
        h_ref[k] = hi
        l_ref[k] = lo
        if f_ref is not None:
            f_ref[k] = out


def rows_kernel(place_ref, row_at_ref, col_at_ref, row_ref, *refs):
    piece_ref, refs = refs[0], refs[1:]
    lows, refs = refs[:2 * LOWS], refs[2 * LOWS:]
    invs, refs = refs[:3 * PARTS], refs[3 * PARTS:]
    shift_ref, child_ref, lead_ref, late_ref, tail_ref, front_ref, out_ref = refs[:7]
    x_ref, f_ref, rh_ref, rl_ref, ch_ref, cl_ref = refs[7:]
    r, c = place_ref[0], place_ref[1]
    side = r // HALF_ROWS
    step = pl.program_id(0)
    blank = jnp.zeros((BS, BS), jnp.bfloat16)

    @pl.when(step == 0)
    def _():
        part = BS // N_ROW
        for i in range(N_ROW):
            x, y = (i + c) % HALF_ROWS, (i // HALF_ROWS) ^ side
            for k in range(PANELS):
                for s in range(COL_SLOTS):
                    at = s * BS + i * part
                    x_ref[k, at:at + part] = piece_ref[x, y, k, s]
        solve_rows(x_ref, None, ch_ref, cl_ref, COL_SLOTS * BS, lows, invs)
        for k in range(PANELS):
            @pl.when(k >= c)
            def _(k=k):
                ch_ref[k, :BS] = blank
                cl_ref[k, :BS] = blank

    @pl.when(step > 0)
    def _():
        rows = ROW_TILE * BS
        for k in range(PANELS):
            for s in range(ROW_TILE):
                x_ref[k, s * BS:(s + 1) * BS] = row_ref[:, k, s].reshape(BS, BS)
        solve_rows(x_ref, f_ref, rh_ref, rl_ref, rows, lows, invs)

        @pl.when(step == 1)
        def _():
            for k in range(PANELS):
                @pl.when(k >= r)
                def _(k=k):
                    rh_ref[k, :BS] = blank
                    rl_ref[k, :BS] = blank
        acc = front_ref[...]
        for k in range(PANELS):
            acc = acc - dot3(rh_ref[k], rl_ref[k], ch_ref[k], cl_ref[k])
        out_ref[...] = acc

        eye = lax.broadcasted_iota(jnp.int32, (BS, BS), 0) == lax.broadcasted_iota(jnp.int32, (BS, BS), 1)
        for s in range(ROW_TILE):
            p = (step - 1) * ROW_TILE + s
            here = slice(s * BS, (s + 1) * BS)
            for t in range(COL_SLOTS):
                there = slice(t * BS, (t + 1) * BS)

                @pl.when(p * N_ROW + r == t * N_COL + c)
                def _(p=p, here=here, there=there):
                    out_ref[here, there] += jnp.where(eye, shift_ref[pl.ds(p * N_ROW + r, 1), :], 0.0)
                for h in range(2):
                    for q in (s, s + 2):
                        for u in (0, 1):
                            if not 0 <= t - u <= 1:
                                continue
                            hit = (row_at_ref[h * CHILD_SLOTS + q] == p) & (col_at_ref[h * 2 + u] == t)

                            @pl.when(hit & (side == h))
                            def _(here=here, there=there, q=q, u=u):
                                out_ref[here, there] += child_ref[q, side, :, u * BS:(u + 1) * BS]

                            @pl.when(hit & (side != h))
                            def _(here=here, there=there, q=q, u=u):
                                if u == 1:
                                    arrived = tail_ref[q]
                                else:
                                    arrived = lead_ref[q] + late_ref[q]
                                out_ref[here, there] += arrived
            level = p * N_ROW + r

            @pl.when((c < PANELS) & (level > c))
            def _(here=here):
                out_ref[here, :BS] = f_ref[c, here]

            for k in range(PANELS):
                @pl.when((c == k) & (level == k))
                def _(here=here, k=k):
                    i, o = part_of(k)
                    out_ref[here, :BS] = invs[3 * i + 2][o]


def finish(place, row_at, col_at, row_panel, col_panel, lows, invs, shift, child, lead, late, tail, front):
    f32, bf = jnp.float32, jnp.bfloat16
    tiles = ROW_SLOTS // ROW_TILE
    whole = pl.BlockSpec(memory_space=pltpu.VMEM)
    smem = pl.BlockSpec(memory_space=pltpu.SMEM)
    tile_at = lambda g: jnp.maximum(g - 1, 0)
    rows, cols = ROW_TILE * BS, COL_SLOTS * BS
    front_spec = pl.BlockSpec((rows, cols), lambda g: (tile_at(g), 0))
    return pl.pallas_call(
        rows_kernel,
        grid=(tiles + 1,),
        in_specs=[smem] * 3
        + [pl.BlockSpec((N_COL, PANELS, ROW_TILE, STRIP, BS), lambda g: (0, 0, tile_at(g), 0, 0))]
        + [whole] * (1 + 2 * LOWS + 3 * PARTS + 5)
        + [front_spec],
        out_specs=front_spec,
        out_shape=jax.ShapeDtypeStruct(front.shape, f32),
        scratch_shapes=[
            pltpu.VMEM((PANELS, cols, BS), f32),
            pltpu.VMEM((PANELS, rows, BS), f32),
            pltpu.VMEM((PANELS, rows, BS), bf),
            pltpu.VMEM((PANELS, rows, BS), bf),
            pltpu.VMEM((PANELS, cols, BS), bf),
            pltpu.VMEM((PANELS, cols, BS), bf),
        ],
        compiler_params=pltpu.CompilerParams(vmem_limit_bytes=60 * 2**20),
        name="finish",
    )(place, row_at, col_at, row_panel, col_panel, *lows, *invs, shift, child, lead, late, tail, front)


def device(r, c):
    return r * N_COL + c


def permute(x, pairs):
    return lax.ppermute(x, ("row", "col"), pairs)


def swap_rows(x, apart, cols):
    return permute(x, [(device(r, c), device(r ^ apart, c)) for r in range(N_ROW) for c in cols])


def after(x, *others):
    return lax.optimization_barrier((x, *others))[0]


def on_device(front_orig, pivot_shift, child_update, child_map):
    r = lax.axis_index("row")
    c = lax.axis_index("col")
    first = r < HALF_ROWS

    child = child_update.reshape(CHILD_SLOTS, 2, BS, 2 * BS)

    def leaving(cols):
        return jnp.where(first, child[:, 1, :, cols], child[:, 0, :, cols])

    lead = leaving(slice(0, BS))
    lead_in = swap_rows(lead, HALF_ROWS, range(PANELS))

    entry = jnp.arange(child_map.shape[1], dtype=jnp.int32)
    want_row = jnp.arange(CHILD_SLOTS, dtype=jnp.int32) * N_ROW + r
    want_col = jnp.arange(2, dtype=jnp.int32) * N_COL + c

    def lookup(wanted):
        hit = wanted[None, :, None] == entry[None, None, :]
        return jnp.sum(jnp.where(hit, child_map[:, None, :], 0), axis=2)

    row_at = lookup(want_row) // N_ROW
    col_at = lookup(want_col) // N_COL

    staying = jnp.where(first, child[:, 0, :, :BS], child[:, 1, :, :BS])
    own = lax.dynamic_index_in_dim(pivot_shift.reshape(ROW_SLOTS, N_ROW, BS), r, axis=1, keepdims=False)
    eye = lax.broadcasted_iota(jnp.int32, (BS, BS), 0) == lax.broadcasted_iota(jnp.int32, (BS, BS), 1)

    def raw_tile(p):
        tile = front_orig[p * BS:(p + 1) * BS, :BS]
        if p == 0:
            tile = tile + jnp.where(eye & (r == c), own[0][:, None], 0.0)
        for h in range(2):
            for q in range(p % 2, CHILD_SLOTS, 2):
                if 0 <= p - q <= 2:
                    part = jnp.where(first == (h == 0), staying[q], lead_in[q])
                    hit = (col_at[h, 0] == 0) & (row_at[h, q] == p)
                    tile = tile + jnp.where(hit, part, 0.0)
        return tile.reshape(N_COL, STRIP, BS)

    def row_gather(x, *groups):
        n = len(groups[0])
        groups = None if n == N_ROW else [list(g) for g in groups]
        return lax.all_to_all(jnp.broadcast_to(x, (n, *x.shape)), "row", 0, 0, axis_index_groups=groups)

    column = jnp.stack([raw_tile(p) for p in range(ROW_SLOTS)], axis=1)
    dealt = lax.all_to_all(column, "col", 0, 0)[:PANELS]

    near = row_gather(dealt[:, 0], range(N_ROW))
    packed = jnp.concatenate([near[i, : i + 1] for i in range(PANELS)], axis=0)
    top = lax.all_gather(packed, "col")
    dealt = after(dealt, packed)

    even, odd = dealt[:, 0::2], dealt[:, 1::2]
    is_odd = c % 2 == 1
    upper = c >= N_ROW

    def turned(flip, far):
        pairs = []
        for i in range(N_ROW):
            for j in range(N_COL):
                to = (j // N_ROW) ^ far
                to = to * HALF_ROWS + (i + j % N_ROW // 2) % HALF_ROWS
                pairs.append((device(i, j), device(to, (j % 2 ^ flip) * N_ROW + i)))
        return permute(jnp.where(is_odd != (flip == 1), odd, even), pairs)

    pair = []
    for far in (0, 1):
        straight, crossed = turned(0, far), turned(1, far)
        pair.append(
            jnp.concatenate([jnp.where(upper, crossed, straight), jnp.where(upper, straight, crossed)], axis=2)
        )
    pair = jnp.stack(pair)
    col_panel = row_gather(pair, range(HALF_ROWS), range(HALF_ROWS, N_ROW))

    row_panel = lax.all_gather(after(dealt, top), "col")

    row_panel = lax.all_gather(dealt, "col")

    lows, invs, blocks = [], [], after(top, pair)
    for i in range(PARTS):
        low, inv, blocks = top_part(CUTS[i], CUTS[i + 1], blocks)
        lows, invs = lows + list(low), invs + list(inv)

    lead_late = swap_rows(after(lead, pair), HALF_ROWS, range(PANELS, N_COL))
    tail_in = swap_rows(after(leaving(slice(BS, 2 * BS)), pair), HALF_ROWS, range(N_COL))

    place = jnp.stack([r, c]).astype(jnp.int32)
    return finish(
        place, row_at.reshape(-1), col_at.reshape(-1), row_panel, col_panel, lows, invs,
        pivot_shift.reshape(-1, BS), child, lead_in, lead_late, tail_in, front_orig,
    )


def solution(mesh):
    in_specs = (P("row", "col"), P(), P("row", "col"), P())
    out_specs = P("row", "col")
    return jax.shard_map(
        on_device, mesh=mesh, in_specs=in_specs, out_specs=out_specs, check_vma=False
    )
```

```python
import jax
import jax.numpy as jnp
from jax import lax
from jax.experimental import pallas as pl
from jax.experimental.pallas import tpu as pltpu
from jax.sharding import PartitionSpec as P

PANELS = 6
BS=256
NT = (((1,), (1,)), ((), ()))
NN = (((1,), (0,)), ((), ()))

def split(x):
    hi = x.astype(jnp.bfloat16)
    return hi, (x - hi.astype(jnp.float32)).astype(jnp.bfloat16)

def dot(a, b, dims=NT):
    return lax.dot_general(a, b, dims, preferred_element_type=jnp.float32)

def dot3(ah, al, bh, bl, dims=NT):
    return dot(ah, bh, dims) + (dot(ah, bl, dims) + dot(al, bh, dims))

def mul3(a, b, dims=NT):
    return dot3(*split(a), *split(b), dims)

def leaf(sym):
    n = sym.shape[0]
    groups = n // 8
    lane = lax.broadcasted_iota(jnp.int32, (8, n), 1)
    sub = lax.broadcasted_iota(jnp.int32, (8, n), 0)
    across = lambda v, j: jnp.broadcast_to(v[:, j:j + 1], (8, n))
    down = lambda v, s: jnp.broadcast_to(v[s:s + 1, :], (8, n))
    rows = [sym[8 * h:8 * h + 8] for h in range(groups)]
    right = [jnp.where(lane == sub + 8 * h, 1.0, 0.0) for h in range(groups)]
    upper, inverse = [], []
    for g in range(groups):
        cols = [across(rows[g], 8 * g + t) for t in range(8)]
        a = {(s, t): down(cols[t], s) for t in range(8) for s in range(t, 8)}
        u = [down(rows[g], t) for t in range(8)]
        w = [down(right[g], t) for t in range(8)]
        later = range(g + 1, groups)
        x = {h: [across(rows[h], 8 * g + t) for t in range(8)] for h in later}
        for t in range(8):
            r = lax.rsqrt(a[t, t])
            for s in range(t + 1, 8):
                a[s, t] = a[s, t] * r
            u[t] = u[t] * r
            w[t] = w[t] * r
            for h in later:
                x[h][t] = x[h][t] * r
            for s in range(t + 1, 8):
                for v in range(t + 1, s + 1):
                    a[s, v] = a[s, v] - a[s, t] * a[v, t]
                u[s] = u[s] - a[s, t] * u[t]
                w[s] = w[s] - a[s, t] * w[t]
                for h in later:
                    x[h][s] = x[h][s] - a[s, t] * x[h][t]
        for h in later:
            for t in range(8):
                rows[h] = rows[h] - x[h][t] * u[t]
                right[h] = right[h] - x[h][t] * w[t]
        ug, wg = u[0], w[0]
        for t in range(1, 8):
            ug = jnp.where(sub == t, u[t], ug)
            wg = jnp.where(sub == t, w[t], wg)
        upper.append(jnp.where(lane >= sub + 8 * g, ug, 0.0))
        inverse.append(wg)
    return jnp.concatenate(upper, axis=0).T, jnp.concatenate(inverse, axis=0)

def symmetric(d):
    n = d.shape[0]
    below = lax.broadcasted_iota(jnp.int32, (n, n), 0) >= lax.broadcasted_iota(jnp.int32, (n, n), 1)
    return jnp.where(below, d, d.T)

LEAF = 128


def low_at(k, i):
    return sum(PANELS - 1 - m for m in range(k)) + i - k - 1


def top_kernel(first, last, in_ref, *refs):
    lh_ref, ll_ref, refs = refs[0], refs[1], refs[2:]
    ih_ref, il_ref, fac_ref, refs = refs[0], refs[1], refs[2], refs[3:]
    if last < PANELS:
        on_ref, refs = refs[0], refs[1:]
    a_ref, s_ref, f_ref, w_ref = refs
    if first == 0:
        e = 0
        for i in range(PANELS):
            for k in range(i + 1):
                a_ref[k * PANELS + i] = in_ref[:, e].reshape(BS, BS)
                e += 1
    else:
        e = 0
        for k in range(first, PANELS):
            a_ref[k * PANELS + k:(k + 1) * PANELS] = in_ref[e:e + PANELS - k]
            e += PANELS - k
    zero = jnp.zeros((LEAF, LEAF), jnp.float32)

    def panel(k, carry):
        d = a_ref[k * PANELS + k]
        s_ref[0] = d[:LEAF, :LEAF]
        s_ref[1] = d[LEAF:, LEAF:]
        s_ref[2] = d[LEAF:, :LEAF]

        def half(h, carry):
            factor, inverse = leaf(symmetric(s_ref[h]))
            f_ref[h] = factor
            w_ref[h] = inverse

            @pl.when(h == 0)
            def _():
                low = mul3(s_ref[2], inverse)
                s_ref[2] = low
                s_ref[1] = s_ref[1] - mul3(low, low)
            return carry
        lax.fori_loop(0, 2, half, 0)
        corner = -mul3(w_ref[1], mul3(s_ref[2], w_ref[0], NN), NN)
        fac_ref[k - first] = jnp.concatenate(
            [jnp.concatenate([f_ref[0], zero], 1), jnp.concatenate([s_ref[2], f_ref[1]], 1)], 0
        )
        inv = jnp.concatenate([jnp.concatenate([w_ref[0], zero], 1), jnp.concatenate([corner, w_ref[1]], 1)], 0)
        ih, il = split(inv)
        ih_ref[k - first] = ih
        il_ref[k - first] = il
        for at in range(first, min(last, PANELS - 1)):
            @pl.when(k == at)
            def _(at=at):
                rest = PANELS - 1 - at
                below = a_ref[at * PANELS + at + 1:(at + 1) * PANELS].reshape(rest * BS, BS)
                xh, xl = split(dot3(*split(below), ih, il))
                lh_ref[low_at(at, at + 1):low_at(at, PANELS)] = xh.reshape(rest, BS, BS)
                ll_ref[low_at(at, at + 1):low_at(at, PANELS)] = xl.reshape(rest, BS, BS)
                for j in range(at + 1, PANELS):
                    o = (j - at - 1) * BS
                    old = a_ref[j * PANELS + j:(j + 1) * PANELS]
                    upd = dot3(xh[o:], xl[o:], xh[o:o + BS], xl[o:o + BS])
                    a_ref[j * PANELS + j:(j + 1) * PANELS] = old - upd.reshape(PANELS - j, BS, BS)
        return carry
    lax.fori_loop(first, last, panel, 0)
    if last < PANELS:
        e = 0
        for k in range(last, PANELS):
            on_ref[e:e + PANELS - k] = a_ref[k * PANELS + k:(k + 1) * PANELS]
            e += PANELS - k


def top_part(first, last, blocks):
    f32, bf = jnp.float32, jnp.bfloat16
    n = last - first
    shapes = [jax.ShapeDtypeStruct((PANELS * (PANELS - 1) // 2, BS, BS), bf)] * 2
    low_count = len(shapes)
    shapes += [jax.ShapeDtypeStruct((n, BS, BS), bf)] * 2 + [jax.ShapeDtypeStruct((n, BS, BS), f32)]
    left = PANELS - last
    if left:
        shapes.append(jax.ShapeDtypeStruct((left * (left + 1) // 2, BS, BS), f32))
    out = pl.pallas_call(
        lambda *refs: top_kernel(first, last, *refs),
        out_shape=shapes,
        scratch_shapes=[
            pltpu.VMEM((PANELS * PANELS, BS, BS), f32),
            pltpu.VMEM((3, LEAF, LEAF), f32),
            pltpu.VMEM((2, LEAF, LEAF), f32),
            pltpu.VMEM((2, LEAF, LEAF), f32),
        ],
        compiler_params=pltpu.CompilerParams(vmem_limit_bytes=40 * 2**20),
        cost_estimate=pl.CostEstimate(flops=n * 11 * 10**9, bytes_accessed=n * 40 * 10**6, transcendentals=n * BS),
        name="top" + str(first),
    )(blocks)
    return out[:low_count], out[low_count:low_count + 3], out[-1] if left else None

HALF_ROWS = 4
N_ROW = 8
N_COL = 16
STRIP = BS // N_COL
ROW_SLOTS = 6
COL_SLOTS = 3
CHILD_SLOTS = 4
ROW_TILE = 2


CUTS = (0, 6)
PARTS = len(CUTS) - 1


def part_of(k):
    i = max(j for j in range(PARTS) if CUTS[j] <= k)
    return i, k - CUTS[i]


def solve_rows(x_ref, f_ref, h_ref, l_ref, rows, lows, invs):
    for k in range(PANELS):
        acc = x_ref[k, :rows]
        for m in range(k):
            acc = acc - dot3(h_ref[m], l_ref[m], lows[0][low_at(m, k)], lows[1][low_at(m, k)])
        i, o = part_of(k)
        out = dot3(*split(acc), invs[3 * i][o], invs[3 * i + 1][o])
        hi, lo = split(out)
        h_ref[k] = hi
        l_ref[k] = lo
        if f_ref is not None:
            f_ref[k] = out


def rows_kernel(place_ref, row_at_ref, col_at_ref, row_ref, *refs):
    piece_ref, refs = refs[0], refs[1:]
    lows, refs = refs[:2], refs[2:]
    invs, refs = refs[:3 * PARTS], refs[3 * PARTS:]
    shift_ref, child_ref, other_ref, front_ref, out_ref = refs[:5]
    x_ref, f_ref, rh_ref, rl_ref, ch_ref, cl_ref = refs[5:]
    r, c = place_ref[0], place_ref[1]
    side = r // HALF_ROWS
    step = pl.program_id(0)
    blank = jnp.zeros((BS, BS), jnp.bfloat16)

    @pl.when(step == 0)
    def _():
        part = BS // N_ROW
        for i in range(N_ROW):
            x, y = (i + c) % HALF_ROWS, (i // HALF_ROWS) ^ side
            for k in range(PANELS):
                for s in range(COL_SLOTS):
                    at = s * BS + i * part
                    x_ref[k, at:at + part] = piece_ref[x, y, k, s]
        solve_rows(x_ref, None, ch_ref, cl_ref, COL_SLOTS * BS, lows, invs)
        for k in range(PANELS):
            @pl.when(k >= c)
            def _(k=k):
                ch_ref[k, :BS] = blank
                cl_ref[k, :BS] = blank

    @pl.when(step > 0)
    def _():
        rows = ROW_TILE * BS
        for k in range(PANELS):
            for s in range(ROW_TILE):
                x_ref[k, s * BS:(s + 1) * BS] = row_ref[:, k, s].reshape(BS, BS)
        solve_rows(x_ref, f_ref, rh_ref, rl_ref, rows, lows, invs)

        @pl.when(step == 1)
        def _():
            for k in range(PANELS):
                @pl.when(k >= r)
                def _(k=k):
                    rh_ref[k, :BS] = blank
                    rl_ref[k, :BS] = blank
        acc = front_ref[...]
        for k in range(PANELS):
            acc = acc - dot3(rh_ref[k], rl_ref[k], ch_ref[k], cl_ref[k])
        out_ref[...] = acc

        eye = lax.broadcasted_iota(jnp.int32, (BS, BS), 0) == lax.broadcasted_iota(jnp.int32, (BS, BS), 1)
        for s in range(ROW_TILE):
            p = (step - 1) * ROW_TILE + s
            here = slice(s * BS, (s + 1) * BS)
            for t in range(COL_SLOTS):
                there = slice(t * BS, (t + 1) * BS)

                @pl.when(p * N_ROW + r == t * N_COL + c)
                def _(p=p, here=here, there=there):
                    out_ref[here, there] += jnp.where(eye, shift_ref[pl.ds(p * N_ROW + r, 1), :], 0.0)
                for h in range(2):
                    for q in (s, s + 2):
                        for u in (0, 1):
                            if not 0 <= t - u <= 1:
                                continue
                            hit = (row_at_ref[h * CHILD_SLOTS + q] == p) & (col_at_ref[h * 2 + u] == t)

                            @pl.when(hit & (side == h))
                            def _(here=here, there=there, q=q, u=u):
                                out_ref[here, there] += child_ref[q, side, :, u * BS:(u + 1) * BS]

                            @pl.when(hit & (side != h))
                            def _(here=here, there=there, q=q, u=u):
                                arrived = other_ref[q, :, u * BS:(u + 1) * BS]
                                out_ref[here, there] += arrived
            level = p * N_ROW + r

            @pl.when((c < PANELS) & (level > c))
            def _(here=here):
                out_ref[here, :BS] = f_ref[c, here]

            for k in range(PANELS):
                @pl.when((c == k) & (level == k))
                def _(here=here, k=k):
                    i, o = part_of(k)
                    out_ref[here, :BS] = invs[3 * i + 2][o]


def finish(place, row_at, col_at, row_panel, col_panel, lows, invs, shift, child, other, front):
    f32, bf = jnp.float32, jnp.bfloat16
    tiles = ROW_SLOTS // ROW_TILE
    whole = pl.BlockSpec(memory_space=pltpu.VMEM)
    smem = pl.BlockSpec(memory_space=pltpu.SMEM)
    tile_at = lambda g: jnp.maximum(g - 1, 0)
    rows, cols = ROW_TILE * BS, COL_SLOTS * BS
    front_spec = pl.BlockSpec((rows, cols), lambda g: (tile_at(g), 0))
    return pl.pallas_call(
        rows_kernel,
        grid=(tiles + 1,),
        in_specs=[smem] * 3
        + [pl.BlockSpec((N_COL, PANELS, ROW_TILE, STRIP, BS), lambda g: (0, 0, tile_at(g), 0, 0))]
        + [whole] * (1 + 2 + 3 * PARTS + 3)
        + [front_spec],
        out_specs=front_spec,
        out_shape=jax.ShapeDtypeStruct(front.shape, f32),
        scratch_shapes=[
            pltpu.VMEM((PANELS, cols, BS), f32),
            pltpu.VMEM((PANELS, rows, BS), f32),
            pltpu.VMEM((PANELS, rows, BS), bf),
            pltpu.VMEM((PANELS, rows, BS), bf),
            pltpu.VMEM((PANELS, cols, BS), bf),
            pltpu.VMEM((PANELS, cols, BS), bf),
        ],
        compiler_params=pltpu.CompilerParams(vmem_limit_bytes=60 * 2**20),
        name="finish",
    )(place, row_at, col_at, row_panel, col_panel, *lows, *invs, shift, child, other, front)


def device(r, c):
    return r * N_COL + c


def permute(x, pairs):
    return lax.ppermute(x, ("row", "col"), pairs)


def swap_rows(x, apart, cols):
    return permute(x, [(device(r, c), device(r ^ apart, c)) for r in range(N_ROW) for c in cols])


def after(x, *others):
    return lax.optimization_barrier((x, *others))[0]


def on_device(front_orig, pivot_shift, child_update, child_map):
    r = lax.axis_index("row")
    c = lax.axis_index("col")
    first = r < HALF_ROWS

    child = child_update.reshape(CHILD_SLOTS, 2, BS, 2 * BS)

    def leaving(cols):
        return jnp.where(first, child[:, 1, :, cols], child[:, 0, :, cols])

    lead = leaving(slice(0, BS))
    lead_in = swap_rows(lead, HALF_ROWS, range(PANELS))

    entry = jnp.arange(child_map.shape[1], dtype=jnp.int32)
    want_row = jnp.arange(CHILD_SLOTS, dtype=jnp.int32) * N_ROW + r
    want_col = jnp.arange(2, dtype=jnp.int32) * N_COL + c

    def lookup(wanted):
        hit = wanted[None, :, None] == entry[None, None, :]
        return jnp.sum(jnp.where(hit, child_map[:, None, :], 0), axis=2)

    row_at = lookup(want_row) // N_ROW
    col_at = lookup(want_col) // N_COL

    staying = jnp.where(first, child[:, 0, :, :BS], child[:, 1, :, :BS])
    own = lax.dynamic_index_in_dim(pivot_shift.reshape(ROW_SLOTS, N_ROW, BS), r, axis=1, keepdims=False)
    eye = lax.broadcasted_iota(jnp.int32, (BS, BS), 0) == lax.broadcasted_iota(jnp.int32, (BS, BS), 1)

    def raw_tile(p):
        tile = front_orig[p * BS:(p + 1) * BS, :BS]
        if p == 0:
            tile = tile + jnp.where(eye & (r == c), own[0][:, None], 0.0)
        for h in range(2):
            for q in range(p % 2, CHILD_SLOTS, 2):
                if 0 <= p - q <= 2:
                    part = jnp.where(first == (h == 0), staying[q], lead_in[q])
                    hit = (col_at[h, 0] == 0) & (row_at[h, q] == p)
                    tile = tile + jnp.where(hit, part, 0.0)
        return tile.reshape(N_COL, STRIP, BS)

    def row_gather(x, *groups):
        n = len(groups[0])
        groups = None if n == N_ROW else [list(g) for g in groups]
        return lax.all_to_all(jnp.broadcast_to(x, (n, *x.shape)), "row", 0, 0, axis_index_groups=groups)

    column = jnp.stack([raw_tile(p) for p in range(ROW_SLOTS)], axis=1)
    dealt = lax.all_to_all(column, "col", 0, 0)[:PANELS]

    other = swap_rows(after(leaving(slice(0, 2 * BS)), dealt), HALF_ROWS, range(N_COL))

    near = row_gather(dealt[:, 0], range(N_ROW))
    packed = jnp.concatenate([near[i, : i + 1] for i in range(PANELS)], axis=0)
    top = lax.all_gather(packed, "col")
    dealt = after(dealt, packed)

    even, odd = dealt[:, 0::2], dealt[:, 1::2]
    is_odd = c % 2 == 1
    upper = c >= N_ROW

    def turned(flip, far):
        pairs = []
        for i in range(N_ROW):
            for j in range(N_COL):
                to = (j // N_ROW) ^ far
                to = to * HALF_ROWS + (i + j % N_ROW // 2) % HALF_ROWS
                pairs.append((device(i, j), device(to, (j % 2 ^ flip) * N_ROW + i)))
        return permute(jnp.where(is_odd != (flip == 1), odd, even), pairs)

    pair = []
    for far in (0, 1):
        straight, crossed = turned(0, far), turned(1, far)
        pair.append(
            jnp.concatenate([jnp.where(upper, crossed, straight), jnp.where(upper, straight, crossed)], axis=2)
        )
    pair = jnp.stack(pair)
    col_panel = row_gather(pair, range(HALF_ROWS), range(HALF_ROWS, N_ROW))

    row_panel = lax.all_gather(after(dealt, top), "col")

    row_panel = lax.all_gather(dealt, "col")

    lows, invs, blocks = [], [], after(top, pair)
    for i in range(PARTS):
        low, inv, blocks = top_part(CUTS[i], CUTS[i + 1], blocks)
        lows, invs = lows + list(low), invs + list(inv)

    place = jnp.stack([r, c]).astype(jnp.int32)
    return finish(
        place, row_at.reshape(-1), col_at.reshape(-1), row_panel, col_panel, lows, invs,
        pivot_shift.reshape(-1, BS), child, other, front_orig,
    )


def solution(mesh):
    in_specs = (P("row", "col"), P(), P("row", "col"), P())
    out_specs = P("row", "col")
    return jax.shard_map(
        on_device, mesh=mesh, in_specs=in_specs, out_specs=out_specs, check_vma=False
    )
```

```python
import jax
import jax.numpy as jnp
from jax import lax
from jax.experimental import pallas as pl
from jax.experimental.pallas import tpu as pltpu
from jax.sharding import PartitionSpec as P

PANELS = 6
BS=256
NT = (((1,), (1,)), ((), ()))
NN = (((1,), (0,)), ((), ()))

def split(x):
    hi = x.astype(jnp.bfloat16)
    return hi, (x - hi.astype(jnp.float32)).astype(jnp.bfloat16)

def dot(a, b, dims=NT):
    return lax.dot_general(a, b, dims, preferred_element_type=jnp.float32)

def dot3(ah, al, bh, bl, dims=NT):
    return dot(ah, bh, dims) + (dot(ah, bl, dims) + dot(al, bh, dims))

def mul3(a, b, dims=NT):
    return dot3(*split(a), *split(b), dims)

def leaf(sym):
    n = sym.shape[0]
    groups = n // 8
    lane = lax.broadcasted_iota(jnp.int32, (8, n), 1)
    sub = lax.broadcasted_iota(jnp.int32, (8, n), 0)
    across = lambda v, j: jnp.broadcast_to(v[:, j:j + 1], (8, n))
    down = lambda v, s: jnp.broadcast_to(v[s:s + 1, :], (8, n))
    rows = [sym[8 * h:8 * h + 8] for h in range(groups)]
    right = [jnp.where(lane == sub + 8 * h, 1.0, 0.0) for h in range(groups)]
    upper, inverse = [], []
    for g in range(groups):
        cols = [across(rows[g], 8 * g + t) for t in range(8)]
        a = {(s, t): down(cols[t], s) for t in range(8) for s in range(t, 8)}
        u = [down(rows[g], t) for t in range(8)]
        w = [down(right[g], t) for t in range(8)]
        later = range(g + 1, groups)
        x = {h: [across(rows[h], 8 * g + t) for t in range(8)] for h in later}
        for t in range(8):
            r = lax.rsqrt(a[t, t])
            for s in range(t + 1, 8):
                a[s, t] = a[s, t] * r
            u[t] = u[t] * r
            w[t] = w[t] * r
            for h in later:
                x[h][t] = x[h][t] * r
            for s in range(t + 1, 8):
                for v in range(t + 1, s + 1):
                    a[s, v] = a[s, v] - a[s, t] * a[v, t]
                u[s] = u[s] - a[s, t] * u[t]
                w[s] = w[s] - a[s, t] * w[t]
                for h in later:
                    x[h][s] = x[h][s] - a[s, t] * x[h][t]
        for h in later:
            for t in range(8):
                rows[h] = rows[h] - x[h][t] * u[t]
                right[h] = right[h] - x[h][t] * w[t]
        ug, wg = u[0], w[0]
        for t in range(1, 8):
            ug = jnp.where(sub == t, u[t], ug)
            wg = jnp.where(sub == t, w[t], wg)
        upper.append(jnp.where(lane >= sub + 8 * g, ug, 0.0))
        inverse.append(wg)
    return jnp.concatenate(upper, axis=0).T, jnp.concatenate(inverse, axis=0)

def symmetric(d):
    n = d.shape[0]
    below = lax.broadcasted_iota(jnp.int32, (n, n), 0) >= lax.broadcasted_iota(jnp.int32, (n, n), 1)
    return jnp.where(below, d, d.T)

LEAF = 128


def low_at(k, i):
    return sum(PANELS - 1 - m for m in range(k)) + i - k - 1


def top_kernel(first, last, in_ref, *refs):
    lh_ref, ll_ref, refs = refs[0], refs[1], refs[2:]
    ih_ref, il_ref, fac_ref, refs = refs[0], refs[1], refs[2], refs[3:]
    if last < PANELS:
        on_ref, refs = refs[0], refs[1:]
    a_ref, s_ref, f_ref, w_ref = refs
    if first == 0:
        e = 0
        for i in range(PANELS):
            for k in range(i + 1):
                a_ref[k * PANELS + i] = in_ref[:, e].reshape(BS, BS)
                e += 1
    else:
        e = 0
        for k in range(first, PANELS):
            a_ref[k * PANELS + k:(k + 1) * PANELS] = in_ref[e:e + PANELS - k]
            e += PANELS - k
    zero = jnp.zeros((LEAF, LEAF), jnp.float32)

    def panel(k, carry):
        d = a_ref[k * PANELS + k]
        s_ref[0] = d[:LEAF, :LEAF]
        s_ref[1] = d[LEAF:, LEAF:]
        s_ref[2] = d[LEAF:, :LEAF]

        def half(h, carry):
            factor, inverse = leaf(symmetric(s_ref[h]))
            f_ref[h] = factor
            w_ref[h] = inverse

            @pl.when(h == 0)
            def _():
                low = mul3(s_ref[2], inverse)
                s_ref[2] = low
                s_ref[1] = s_ref[1] - mul3(low, low)
            return carry
        lax.fori_loop(0, 2, half, 0)
        corner = -mul3(w_ref[1], mul3(s_ref[2], w_ref[0], NN), NN)
        fac_ref[k - first] = jnp.concatenate(
            [jnp.concatenate([f_ref[0], zero], 1), jnp.concatenate([s_ref[2], f_ref[1]], 1)], 0
        )
        inv = jnp.concatenate([jnp.concatenate([w_ref[0], zero], 1), jnp.concatenate([corner, w_ref[1]], 1)], 0)
        ih, il = split(inv)
        ih_ref[k - first] = ih
        il_ref[k - first] = il
        for at in range(first, min(last, PANELS - 1)):
            @pl.when(k == at)
            def _(at=at):
                rest = PANELS - 1 - at
                below = a_ref[at * PANELS + at + 1:(at + 1) * PANELS].reshape(rest * BS, BS)
                xh, xl = split(dot3(*split(below), ih, il))
                lh_ref[low_at(at, at + 1):low_at(at, PANELS)] = xh.reshape(rest, BS, BS)
                ll_ref[low_at(at, at + 1):low_at(at, PANELS)] = xl.reshape(rest, BS, BS)
                for j in range(at + 1, PANELS):
                    o = (j - at - 1) * BS
                    old = a_ref[j * PANELS + j:(j + 1) * PANELS]
                    upd = dot3(xh[o:], xl[o:], xh[o:o + BS], xl[o:o + BS])
                    a_ref[j * PANELS + j:(j + 1) * PANELS] = old - upd.reshape(PANELS - j, BS, BS)
        return carry
    lax.fori_loop(first, last, panel, 0)
    if last < PANELS:
        e = 0
        for k in range(last, PANELS):
            on_ref[e:e + PANELS - k] = a_ref[k * PANELS + k:(k + 1) * PANELS]
            e += PANELS - k


def top_part(first, last, blocks):
    f32, bf = jnp.float32, jnp.bfloat16
    n = last - first
    shapes = [jax.ShapeDtypeStruct((PANELS * (PANELS - 1) // 2, BS, BS), bf)] * 2
    low_count = len(shapes)
    shapes += [jax.ShapeDtypeStruct((n, BS, BS), bf)] * 2 + [jax.ShapeDtypeStruct((n, BS, BS), f32)]
    left = PANELS - last
    if left:
        shapes.append(jax.ShapeDtypeStruct((left * (left + 1) // 2, BS, BS), f32))
    out = pl.pallas_call(
        lambda *refs: top_kernel(first, last, *refs),
        out_shape=shapes,
        out_specs=[pl.BlockSpec(memory_space=pltpu.VMEM)] * len(shapes),
        scratch_shapes=[
            pltpu.VMEM((PANELS * PANELS, BS, BS), f32),
            pltpu.VMEM((3, LEAF, LEAF), f32),
            pltpu.VMEM((2, LEAF, LEAF), f32),
            pltpu.VMEM((2, LEAF, LEAF), f32),
        ],
        compiler_params=pltpu.CompilerParams(vmem_limit_bytes=40 * 2**20),
        cost_estimate=pl.CostEstimate(flops=n * 11 * 10**9, bytes_accessed=n * 40 * 10**6, transcendentals=n * BS),
        name="top" + str(first),
    )(blocks)
    return out[:low_count], out[low_count:low_count + 3], out[-1] if left else None

HALF_ROWS = 4
N_ROW = 8
N_COL = 16
STRIP = BS // N_COL
ROW_SLOTS = 6
COL_SLOTS = 3
CHILD_SLOTS = 4
ROW_TILE = 2


CUTS = (0, 6)
PARTS = len(CUTS) - 1


def part_of(k):
    i = max(j for j in range(PARTS) if CUTS[j] <= k)
    return i, k - CUTS[i]


def solve_rows(x_ref, f_ref, h_ref, l_ref, rows, lows, invs):
    for k in range(PANELS):
        acc = x_ref[k, :rows]
        for m in range(k):
            acc = acc - dot3(h_ref[m], l_ref[m], lows[0][low_at(m, k)], lows[1][low_at(m, k)])
        i, o = part_of(k)
        out = dot3(*split(acc), invs[3 * i][o], invs[3 * i + 1][o])
        hi, lo = split(out)
        h_ref[k] = hi
        l_ref[k] = lo
        if f_ref is not None:
            f_ref[k] = out


def rows_kernel(place_ref, row_at_ref, col_at_ref, row_ref, *refs):
    piece_ref, refs = refs[0], refs[1:]
    lows, refs = refs[:2], refs[2:]
    invs, refs = refs[:3 * PARTS], refs[3 * PARTS:]
    shift_ref, child_ref, other_ref, front_ref, out_ref = refs[:5]
    x_ref, f_ref, rh_ref, rl_ref, ch_ref, cl_ref = refs[5:]
    r, c = place_ref[0], place_ref[1]
    side = r // HALF_ROWS
    step = pl.program_id(0)
    blank = jnp.zeros((BS, BS), jnp.bfloat16)

    @pl.when(step == 0)
    def _():
        part = BS // N_ROW
        for i in range(N_ROW):
            x, y = (i + c) % HALF_ROWS, (i // HALF_ROWS) ^ side
            for k in range(PANELS):
                for s in range(COL_SLOTS):
                    at = s * BS + i * part
                    x_ref[k, at:at + part] = piece_ref[x, y, k, s]
        solve_rows(x_ref, None, ch_ref, cl_ref, COL_SLOTS * BS, lows, invs)
        for k in range(PANELS):
            @pl.when(k >= c)
            def _(k=k):
                ch_ref[k, :BS] = blank
                cl_ref[k, :BS] = blank

    @pl.when(step > 0)
    def _():
        rows = ROW_TILE * BS
        for k in range(PANELS):
            for s in range(ROW_TILE):
                x_ref[k, s * BS:(s + 1) * BS] = row_ref[:, k, s].reshape(BS, BS)
        solve_rows(x_ref, f_ref, rh_ref, rl_ref, rows, lows, invs)

        @pl.when(step == 1)
        def _():
            for k in range(PANELS):
                @pl.when(k >= r)
                def _(k=k):
                    rh_ref[k, :BS] = blank
                    rl_ref[k, :BS] = blank
        acc = front_ref[...]
        for k in range(PANELS):
            acc = acc - dot3(rh_ref[k], rl_ref[k], ch_ref[k], cl_ref[k])
        out_ref[...] = acc

        eye = lax.broadcasted_iota(jnp.int32, (BS, BS), 0) == lax.broadcasted_iota(jnp.int32, (BS, BS), 1)
        for s in range(ROW_TILE):
            p = (step - 1) * ROW_TILE + s
            here = slice(s * BS, (s + 1) * BS)
            for t in range(COL_SLOTS):
                there = slice(t * BS, (t + 1) * BS)

                @pl.when(p * N_ROW + r == t * N_COL + c)
                def _(p=p, here=here, there=there):
                    out_ref[here, there] += jnp.where(eye, shift_ref[pl.ds(p * N_ROW + r, 1), :], 0.0)
                for h in range(2):
                    for q in (s, s + 2):
                        for u in (0, 1):
                            if not 0 <= t - u <= 1:
                                continue
                            hit = (row_at_ref[h * CHILD_SLOTS + q] == p) & (col_at_ref[h * 2 + u] == t)

                            @pl.when(hit & (side == h))
                            def _(here=here, there=there, q=q, u=u):
                                out_ref[here, there] += child_ref[q, side, :, u * BS:(u + 1) * BS]

                            @pl.when(hit & (side != h))
                            def _(here=here, there=there, q=q, u=u):
                                arrived = other_ref[q, :, u * BS:(u + 1) * BS]
                                out_ref[here, there] += arrived
            level = p * N_ROW + r

            @pl.when((c < PANELS) & (level > c))
            def _(here=here):
                out_ref[here, :BS] = f_ref[c, here]

            for k in range(PANELS):
                @pl.when((c == k) & (level == k))
                def _(here=here, k=k):
                    i, o = part_of(k)
                    out_ref[here, :BS] = invs[3 * i + 2][o]


def finish(place, row_at, col_at, row_panel, col_panel, lows, invs, shift, child, other, front):
    f32, bf = jnp.float32, jnp.bfloat16
    tiles = ROW_SLOTS // ROW_TILE
    whole = pl.BlockSpec(memory_space=pltpu.VMEM)
    smem = pl.BlockSpec(memory_space=pltpu.SMEM)
    tile_at = lambda g: jnp.maximum(g - 1, 0)
    rows, cols = ROW_TILE * BS, COL_SLOTS * BS
    front_spec = pl.BlockSpec((rows, cols), lambda g: (tile_at(g), 0))
    return pl.pallas_call(
        rows_kernel,
        grid=(tiles + 1,),
        in_specs=[smem] * 3
        + [pl.BlockSpec((N_COL, PANELS, ROW_TILE, STRIP, BS), lambda g: (0, 0, tile_at(g), 0, 0))]
        + [whole] * (1 + 2 + 3 * PARTS + 3)
        + [front_spec],
        out_specs=front_spec,
        out_shape=jax.ShapeDtypeStruct(front.shape, f32),
        scratch_shapes=[
            pltpu.VMEM((PANELS, cols, BS), f32),
            pltpu.VMEM((PANELS, rows, BS), f32),
            pltpu.VMEM((PANELS, rows, BS), bf),
            pltpu.VMEM((PANELS, rows, BS), bf),
            pltpu.VMEM((PANELS, cols, BS), bf),
            pltpu.VMEM((PANELS, cols, BS), bf),
        ],
        compiler_params=pltpu.CompilerParams(vmem_limit_bytes=60 * 2**20),
        name="finish",
    )(place, row_at, col_at, row_panel, col_panel, *lows, *invs, shift, child, other, front)


def device(r, c):
    return r * N_COL + c


def permute(x, pairs):
    return lax.ppermute(x, ("row", "col"), pairs)


def swap_rows(x, apart, cols):
    return permute(x, [(device(r, c), device(r ^ apart, c)) for r in range(N_ROW) for c in cols])


def after(x, *others):
    return lax.optimization_barrier((x, *others))[0]


def on_device(front_orig, pivot_shift, child_update, child_map):
    r = lax.axis_index("row")
    c = lax.axis_index("col")
    first = r < HALF_ROWS

    child = child_update.reshape(CHILD_SLOTS, 2, BS, 2 * BS)

    def leaving(cols):
        return jnp.where(first, child[:, 1, :, cols], child[:, 0, :, cols])

    lead = leaving(slice(0, BS))
    lead_in = swap_rows(lead, HALF_ROWS, range(PANELS))

    entry = jnp.arange(child_map.shape[1], dtype=jnp.int32)
    want_row = jnp.arange(CHILD_SLOTS, dtype=jnp.int32) * N_ROW + r
    want_col = jnp.arange(2, dtype=jnp.int32) * N_COL + c

    def lookup(wanted):
        hit = wanted[None, :, None] == entry[None, None, :]
        return jnp.sum(jnp.where(hit, child_map[:, None, :], 0), axis=2)

    row_at = lookup(want_row) // N_ROW
    col_at = lookup(want_col) // N_COL

    staying = jnp.where(first, child[:, 0, :, :BS], child[:, 1, :, :BS])
    own = lax.dynamic_index_in_dim(pivot_shift.reshape(ROW_SLOTS, N_ROW, BS), r, axis=1, keepdims=False)
    eye = lax.broadcasted_iota(jnp.int32, (BS, BS), 0) == lax.broadcasted_iota(jnp.int32, (BS, BS), 1)

    def raw_tile(p):
        tile = front_orig[p * BS:(p + 1) * BS, :BS]
        if p == 0:
            tile = tile + jnp.where(eye & (r == c), own[0][:, None], 0.0)
        for h in range(2):
            for q in range(p % 2, CHILD_SLOTS, 2):
                if 0 <= p - q <= 2:
                    part = jnp.where(first == (h == 0), staying[q], lead_in[q])
                    hit = (col_at[h, 0] == 0) & (row_at[h, q] == p)
                    tile = tile + jnp.where(hit, part, 0.0)
        return tile.reshape(N_COL, STRIP, BS)

    def row_gather(x, *groups):
        n = len(groups[0])
        groups = None if n == N_ROW else [list(g) for g in groups]
        return lax.all_to_all(jnp.broadcast_to(x, (n, *x.shape)), "row", 0, 0, axis_index_groups=groups)

    column = jnp.stack([raw_tile(p) for p in range(ROW_SLOTS)], axis=1)
    dealt = lax.all_to_all(column, "col", 0, 0)[:PANELS]

    near = row_gather(dealt[:, 0], range(N_ROW))
    packed = jnp.concatenate([near[i, : i + 1] for i in range(PANELS)], axis=0)
    top = lax.all_gather(packed, "col")
    dealt = after(dealt, packed)

    even, odd = dealt[:, 0::2], dealt[:, 1::2]
    is_odd = c % 2 == 1
    upper = c >= N_ROW

    def turned(flip, far):
        pairs = []
        for i in range(N_ROW):
            for j in range(N_COL):
                to = (j // N_ROW) ^ far
                to = to * HALF_ROWS + (i + j % N_ROW // 2) % HALF_ROWS
                pairs.append((device(i, j), device(to, (j % 2 ^ flip) * N_ROW + i)))
        return permute(jnp.where(is_odd != (flip == 1), odd, even), pairs)

    pair = []
    for far in (0, 1):
        straight, crossed = turned(0, far), turned(1, far)
        pair.append(
            jnp.concatenate([jnp.where(upper, crossed, straight), jnp.where(upper, straight, crossed)], axis=2)
        )
    pair = jnp.stack(pair)
    col_panel = row_gather(pair, range(HALF_ROWS), range(HALF_ROWS, N_ROW))

    other = swap_rows(after(leaving(slice(0, 2 * BS)), pair), HALF_ROWS, range(N_COL))

    row_panel = lax.all_gather(after(dealt, top), "col")

    row_panel = lax.all_gather(dealt, "col")

    lows, invs, blocks = [], [], after(top, pair)
    for i in range(PARTS):
        low, inv, blocks = top_part(CUTS[i], CUTS[i + 1], blocks)
        lows, invs = lows + list(low), invs + list(inv)

    place = jnp.stack([r, c]).astype(jnp.int32)
    return finish(
        place, row_at.reshape(-1), col_at.reshape(-1), row_panel, col_panel, lows, invs,
        pivot_shift.reshape(-1, BS), child, other, front_orig,
    )


def solution(mesh):
    in_specs = (P("row", "col"), P(), P("row", "col"), P())
    out_specs = P("row", "col")
    return jax.shard_map(
        on_device, mesh=mesh, in_specs=in_specs, out_specs=out_specs, check_vma=False
    )
```
